768 devices in a mesh: lat: 48 (over x_hi, z, core), lon: 16 (over x_lo, y).
Axes of the slice: x: 4 (x_hi: 2, x_lo: 2; x = x_hi * 2 + x_lo), y: 8, z: 12, core: 2. Of those that a mesh axis runs over, the one named last changes fastest.
Arguments:
- tokens: bfloat16 [4, 288, 384, 192], P(None, 'lat', 'lon'), may hold values from -6 to 6
- cotangent: bfloat16 [4, 288, 384, 192], P(None, 'lat', 'lon'), may hold values from -6 to 6
- norm_gain: float32 [192], replicated, may hold values from 0.1 to 1.9
- inproj_weight: bfloat16 [192, 576], replicated, may hold values from -0.4375 to 0.4375
- outproj_weight: bfloat16 [192, 192], replicated, may hold values from -0.4375 to 0.4375
- bias: float32 [2, 48, 6, 144, 144], P(None, 'lat'), may hold values from -4 to 4
Outputs:
- grad_input: bfloat16 [4, 288, 384, 192], P(None, 'lat', 'lon')
- bias_grad: float32 [2, 48, 6, 144, 144], P(None, 'lat', None, 'lon')
The draws below stay inside these ranges and needn't reach their ends.
All inputs are finite; a program needn't handle non-finite values.
Results may differ from the reference program's by a relative error of at most 0.017.
Values may be sent and summed in bfloat16 or wider, within the bound.
A program may use at most 32 MiB of HBM per device.

```python
import jax
import jax.numpy as jnp
from jax import lax

C = 192
HEADS = 6
WZ = 2
WH = 6
WW = 12
WT = 144
ZWIN = 2
LATW = 48
LONW = 32
LEVELS = 4
ROWS = 288
COLS = 384


def steps_of(stream_key, dims, pieces, low, largest):
    level, own = 1.0, jax.random.fold_in(stream_key, 6)
    for axis_at, shards_of in pieces:
        heights = jnp.exp(jax.random.uniform(jax.random.fold_in(own, axis_at), (shards_of,), jnp.float32, low / len(pieces), largest / len(pieces)))
        level = level * jnp.repeat(heights, dims[axis_at] // shards_of).reshape([-1 if axis == axis_at else 1 for axis in range(len(dims))])
    return level


def bell_draw(key, extent, scale, most, shards=(), kind=jnp.bfloat16):
    array = jax.random.normal(key, extent, jnp.float32) * scale
    if len(shards) > 0:
        array = steps_of(key, extent, shards, -0.22, 0.18) * array
    return jnp.clip(array, min=-most, max=most).astype(kind)


def setup_inputs(seed: int = 0) -> dict:
    keys = jax.random.split(jax.random.key(seed), 7)
    return {
        "tokens": bell_draw(keys[0], (LEVELS, ROWS, COLS, C), 1.0, 6.0, ((1, 48), (2, 16))),
        "cotangent": bell_draw(keys[1], (LEVELS, ROWS, COLS, C), 2.0, 6.0, ((1, 48), (2, 16))),
        "norm_gain": jnp.clip(1.0 + 0.18 * jax.random.normal(keys[2], (C,), jnp.float32), 0.1, 1.9),
        "inproj_weight": bell_draw(keys[3], (C, 3 * C), C ** -0.5, 0.4375),
        "outproj_weight": bell_draw(keys[4], (C, C), C ** -0.5, 0.4375),
        "bias": bell_draw(keys[5], (ZWIN, LATW, HEADS, WT, WT), 1.0, 4.0, ((1, 48),), jnp.float32),
    }


epsilon = 1e-05

def allowed_pairs(level_win, lat_window, level_total, row_total):
    positions = jnp.arange(WZ * WH * WW, dtype=jnp.int32)
    level_pos = level_win * WZ + positions // (WH * WW)
    row_pos = lat_window * WH + positions // WW % WH
    labels = (level_pos >= level_total - WZ // 2).astype(jnp.int32) * 2 + (row_pos >= row_total - WH // 2).astype(jnp.int32)
    return labels[:, None] == labels[None, :]

def to_windows(field):
    level_total, row_total, col_total, channels = field.shape
    blocks = field.reshape(level_total // WZ, WZ, row_total // WH, WH, col_total // WW, WW, channels)
    blocks = blocks.transpose(0, 2, 4, 1, 3, 5, 6)
    return blocks.reshape(level_total // WZ, row_total // WH, col_total // WW, WZ * WH * WW, channels)

def from_windows(blocks):
    level_win, lat_win, lon_win, token_count, channels = blocks.shape
    field = blocks.reshape(level_win, lat_win, lon_win, WZ, WH, WW, channels)
    field = field.transpose(0, 3, 1, 4, 2, 5, 6)
    return field.reshape(level_win * WZ, lat_win * WH, lon_win * WW, channels)

def band_backward(band_in, band_grad, gain, inproj_weight, outproj_weight, band_bias, allowed):
    window_count, token_count, channels = band_in.shape
    head_count = band_bias.shape[0]
    head_dim = channels // head_count
    scaling = head_dim ** (-0.5)
    floats = band_in.astype(jnp.float32)
    centred = floats - lax.optimization_barrier(jnp.mean(floats, axis=-1, keepdims=True))
    inverse_rms = lax.rsqrt(lax.optimization_barrier(jnp.mean(centred * centred, axis=-1, keepdims=True)) + epsilon)
    standard = centred * inverse_rms
    normed = (standard * gain.astype(jnp.float32)).astype(jnp.bfloat16)
    projected = jnp.dot(normed.reshape(-1, channels), inproj_weight, preferred_element_type=jnp.float32).astype(jnp.bfloat16)
    projected = projected.reshape(window_count, token_count, 3, head_count, head_dim).astype(jnp.float32)
    query_rows = projected[:, :, 0]
    key_rows = projected[:, :, 1]
    value_rows = projected[:, :, 2]
    scores = jnp.einsum('nihd,njhd->nhij', query_rows, key_rows) * scaling + band_bias[None].astype(jnp.float32)
    weights = jnp.where(allowed[None, None], jnp.exp(scores), 0.0)
    probabilities = weights / lax.optimization_barrier(jnp.sum(weights, axis=-1, keepdims=True))
    upstream = jnp.dot(band_grad.reshape(-1, channels), outproj_weight.T, preferred_element_type=jnp.float32).astype(jnp.bfloat16)
    upstream = upstream.reshape(window_count, token_count, head_count, head_dim).astype(jnp.float32)
    dprobs = jnp.einsum('nihd,njhd->nhij', upstream, value_rows)
    inner_sum = lax.optimization_barrier(jnp.sum(probabilities * dprobs, axis=-1, keepdims=True))
    dscores = probabilities * (dprobs - inner_sum)
    bias_part = lax.optimization_barrier(jnp.sum(dscores, axis=0))
    probs_low = probabilities.astype(jnp.bfloat16).astype(jnp.float32)
    dscores_low = dscores.astype(jnp.bfloat16).astype(jnp.float32)
    dquery = (jnp.einsum('nhij,njhd->nihd', dscores_low, key_rows) * scaling).astype(jnp.bfloat16)
    dkeys = (jnp.einsum('nhij,nihd->njhd', dscores_low, query_rows) * scaling).astype(jnp.bfloat16)
    dvalues = jnp.einsum('nhij,nihd->njhd', probs_low, upstream).astype(jnp.bfloat16)
    dprojected = jnp.stack([dquery, dkeys, dvalues], axis=2).reshape(-1, 3 * channels)
    dnormed = jnp.dot(dprojected, inproj_weight.T, preferred_element_type=jnp.float32)
    dnormed = dnormed.reshape(window_count, token_count, channels)
    scaled = dnormed * gain.astype(jnp.float32)
    grad_moved = inverse_rms * (scaled - lax.optimization_barrier(jnp.mean(scaled, axis=-1, keepdims=True)) - standard * lax.optimization_barrier(jnp.mean(scaled * standard, axis=-1, keepdims=True)))
    return (grad_moved.astype(jnp.bfloat16), bias_part)

def reference(tokens, cotangent, norm_gain, inproj_weight, outproj_weight, bias):
    forward_shift = (-(WZ // 2), -(WH // 2), -(WW // 2))
    moved = jnp.roll(tokens, forward_shift, axis=(0, 1, 2))
    moved_grad = jnp.roll(cotangent, forward_shift, axis=(0, 1, 2))
    in_windows = to_windows(moved).reshape(ZWIN * LATW, LONW, WT, C)
    grad_windows = to_windows(moved_grad).reshape(ZWIN * LATW, LONW, WT, C)
    bias_flat = bias.reshape(ZWIN * LATW, HEADS, WT, WT)
    band_ids = jnp.arange(ZWIN * LATW, dtype=jnp.int32)

    def one_band(operands):
        band_in, band_grad, band_bias, band_id = operands
        allowed = allowed_pairs(band_id // LATW, band_id % LATW, LEVELS, ROWS)
        return band_backward(band_in, band_grad, norm_gain, inproj_weight, outproj_weight, band_bias, allowed)
    grad_blocks, bias_parts = lax.map(one_band, (in_windows, grad_windows, bias_flat, band_ids))
    grad_field = from_windows(grad_blocks.reshape(ZWIN, LATW, LONW, WT, C))
    grad_input = jnp.roll(grad_field, (WZ // 2, WH // 2, WW // 2), axis=(0, 1, 2))
    return (grad_input, bias_parts.reshape(ZWIN, LATW, HEADS, WT, WT))
```

```python
import jax
import jax.numpy as jnp
from jax import lax
from jax.experimental import pallas as pl
from jax.experimental.pallas import tpu as pltpu
from jax.sharding import PartitionSpec as P

EPS = 1e-05
HEADS = 6
C = 192
LOG2E = 1.4426950408889634
SCALE = 32 ** (-0.5)
BF = jnp.bfloat16
F32 = jnp.float32
OWNERS = 16
LANES = 64 * OWNERS
GROUPS = ((1, 0, 2), (3, 2, 1), (0, 3, 1))
MESH = pl.DeviceIdType.MESH


def nn(a, b):
    return lax.dot_general(a, b, (((1,), (0,)), ((), ())), preferred_element_type=F32)


def nt(a, b):
    return lax.dot_general(a, b, (((1,), (1,)), ((), ())), preferred_element_type=F32)


def tn(a, b):
    return lax.dot_general(a, b, (((0,), (0,)), ((), ())), preferred_element_type=F32)


def iota(shape, dim):
    return lax.broadcasted_iota(jnp.int32, shape, dim)


def one_hot(cond):
    return jnp.where(cond, 1.0, 0.0).astype(BF)


def lane_head(shape):
    return ((iota(shape, 1) & 63) * 57) >> 9


def lane_query(shape):
    lane = iota(shape, 1)
    inner = lane & 63
    return 9 * (lane >> 6) + inner - 9 * ((inner * 57) >> 9)


def make_kernel(lat_count, lon_count):
    def kernel(
        tok, cot, gain_ref, win_ref, wout_ref, bias_ref, out_ref, bout_ref,
        x, bias_v, bt0, bt1, sel, mask, pc, pct, wq, wk, wv, wqt, wkt,
        ext, sb0, sb1, rb0, rb1, rl, rc, rd,
        bias_sem, own_sem, hs_sem, hr_sem, bs_sem, br_sem, gs_sem, gr_sem,
    ):
        lat = lax.axis_index("lat")
        lon = lax.axis_index("lon")
        lat_next = lax.rem(lat + 1, lat_count)
        lat_prev = lax.rem(lat + lat_count - 1, lat_count)
        lon_next = lax.rem(lon + 1, lon_count)
        lon_prev = lax.rem(lon + lon_count - 1, lon_count)

        barrier = pltpu.get_barrier_semaphore()

        def greet(r, carry):
            pl.semaphore_signal(
                barrier, inc=1, device_id=(lat, lax.rem(lon + r, lon_count)), device_id_type=MESH
            )
            return carry

        for there in ((lat_prev, lon), (lat_next, lon), (lat_prev, lon_prev), (lat_next, lon_next)):
            pl.semaphore_signal(barrier, inc=1, device_id=there, device_id_type=MESH)
        lax.fori_loop(1, lon_count, greet, 0)

        bias_copies = [
            pltpu.make_async_copy(bias_ref.at[a], bias_v.at[a], bias_sem.at[a]) for a in range(2)
        ]
        for copy in bias_copies:
            copy.start()
        own_copies = []
        for which, ref in enumerate((tok, cot)):
            for g, (src, z, count) in enumerate(GROUPS):
                own_copies.append(
                    pltpu.make_async_copy(
                        ref.at[src : src + count, 3:6],
                        x.at[which, z : z + count, 0:3, 0:3],
                        own_sem.at[which, g],
                    )
                )
                own_copies[-1].start()

        sel[...] = one_hot((iota((144, LANES), 0) == lane_query((144, LANES))) & (lane_head((144, LANES)) < HEADS))
        mask[...] = one_hot((iota((C, LANES), 0) >> 5) == lane_head((C, LANES)))
        for c in range(2):
            p = iota((72, 192), 0)
            row = (p * 43) >> 9
            pc[c] = one_hot(iota((72, 192), 1) == 32 * row + p - 12 * row + 6 + 12 * c)
            p = iota((192, 72), 1)
            row = (p * 43) >> 9
            pct[c] = one_hot(iota((192, 72), 0) == 32 * row + p - 12 * row + 6 + 12 * c)
        wq[...] = win_ref[:, 0:192]
        wk[...] = win_ref[:, 192:384]
        wv[...] = win_ref[:, 384:576]
        wqt[...] = wq[...].astype(F32).T.astype(BF)
        wkt[...] = wk[...].astype(F32).T.astype(BF)

        pl.semaphore_wait(barrier, lon_count - 1 + 4)

        halo_copies = [[], [], []]
        for g, (src, z, count) in enumerate(GROUPS):
            for which, ref in enumerate((tok, cot)):
                for kind, (source, target, there) in enumerate(
                    (
                        (ref.at[src : src + count, 0:3], x.at[which, z : z + count, 3:6, 0:3], (lat_prev, lon)),
                        (ref.at[src : src + count, 0:3, 0], x.at[which, z : z + count, 3:6, 3], (lat_prev, lon_prev)),
                        (ref.at[src : src + count, 3:6, 0], x.at[which, z : z + count, 0:3, 3], (lat, lon_prev)),
                    )
                ):
                    copy = pltpu.make_async_remote_copy(
                        src_ref=source,
                        dst_ref=target,
                        send_sem=hs_sem.at[which, kind, g],
                        recv_sem=hr_sem.at[which, kind, g],
                        device_id=there,
                        device_id_type=MESH,
                    )
                    copy.start()
                    halo_copies[g].append(copy)

        is_last = jnp.where(lat == lat_count - 1, -1e30, 0.0).astype(F32)

        def penalty(rows):
            key_late = lax.rem(iota((rows, 1), 0), 72) >= 36
            query_late = lax.rem(lane_query((1, 64 * rows // 9)), 72) >= 36
            return jnp.where(key_late != query_late, is_last, 0.0)

        for a in range(2):
            bias_copies[a].wait()
        heads0 = lane_head((1, LANES))
        total = jnp.zeros((144, LANES), F32)
        for h in range(HEADS):
            b = bias_v[0, 144 * h : 144 * h + 144, :] * LOG2E
            high = b.astype(BF)
            low = (b - high.astype(F32)).astype(BF)
            moved = tn(high, sel[...]) + tn(low, sel[...])
            total = jnp.where(heads0 == h, moved, total)
        bt0[...] = total + penalty(144)
        heads1 = lane_head((1, LANES // 2))
        for s in range(2):
            total = jnp.zeros((72, LANES // 2), F32)
            for h in range(HEADS):
                b = bias_v[1, 144 * h + 72 * s : 144 * h + 72 * s + 72, :] * LOG2E
                high = b.astype(BF)
                low = (b - high.astype(F32)).astype(BF)
                half = sel[0:72, 0 : LANES // 2]
                moved = (tn(high, half) + tn(low, half))[72 * s : 72 * s + 72]
                total = jnp.where(heads1 == h, moved, total)
            bt1[s] = total + penalty(72)

        gain = gain_ref[...]

        def segment(t, ct, biast, choose, block):
            centred = t - jnp.sum(t, axis=-1, keepdims=True) * (1.0 / C)
            inverse = lax.rsqrt(jnp.sum(centred * centred, axis=-1, keepdims=True) * (1.0 / C) + EPS)
            standard = centred * inverse
            normed = (standard * gain).astype(BF)
            qt = nt(wqt[...], normed).astype(BF)
            kt = nt(wkt[...], normed).astype(BF)
            k = nn(normed, wk[...]).astype(BF)
            v = nn(normed, wv[...]).astype(BF)
            ut = nt(wout_ref[...], ct).astype(BF)
            qbd = nn(qt, choose).astype(BF) * block
            ubd = nn(ut, choose).astype(BF) * block
            e = jnp.exp2(nn(k, qbd) * (SCALE * LOG2E) + biast)
            probs = e * (1.0 / jnp.sum(e, axis=0, keepdims=True))
            dprobs = nn(v, ubd)
            inner = jnp.sum(probs * dprobs, axis=0, keepdims=True)
            dscores = probs * (dprobs - inner)
            p_low = probs.astype(BF)
            d_low = dscores.astype(BF)
            dv = nt(p_low, ubd).astype(BF)
            dk = (nt(d_low, qbd) * SCALE).astype(BF)
            wide = (nn(kt, d_low) * SCALE).astype(BF) * block
            dq = nt(choose, wide).astype(BF)
            dnormed = nt(dq, wq[...]) + nt(dk, wk[...]) + nt(dv, wv[...])
            scaled = dnormed * gain
            grad = inverse * (
                scaled
                - jnp.sum(scaled, axis=-1, keepdims=True) * (1.0 / C)
                - standard * (jnp.sum(scaled * standard, axis=-1, keepdims=True) * (1.0 / C))
            )
            return grad, dscores

        lane = iota((1, 128), 1) < 64

        def load_level(which, z):
            return x[which, z].reshape(192, C)

        def store_level(z, parts):
            full = nn(pct[0], parts[0].astype(BF)) + nn(pct[1], parts[1].astype(BF))
            ext[z] = full.reshape(6, 4, 8, C).astype(BF)

        def send_grads(a):
            copies = []
            span = pl.ds(2 * a, 2)
            for kind, (source, target, there) in enumerate(
                (
                    (ext.at[span, 3:6, 0:3], rl.at[span], (lat_next, lon)),
                    (ext.at[span, 3:6, 3], rd.at[span], (lat_next, lon_next)),
                    (ext.at[span, 0:3, 3], rc.at[span], (lat, lon_next)),
                )
            ):
                copy = pltpu.make_async_remote_copy(
                    src_ref=source,
                    dst_ref=target,
                    send_sem=gs_sem.at[a, kind],
                    recv_sem=gr_sem.at[a, kind],
                    device_id=there,
                    device_id_type=MESH,
                )
                copy.start()
                copies.append(copy)
            return copies

        def bias_copy(a, r):
            there = lax.rem(lon + r, lon_count)
            source, target = ((sb0, rb0), (sb1, rb1))[a]
            return pltpu.make_async_remote_copy(
                src_ref=source.at[there],
                dst_ref=target.at[r],
                send_sem=bs_sem.at[a, r],
                recv_sem=br_sem.at[a, r],
                device_id=(lat, there),
                device_id_type=MESH,
            )

        def send_bias(a):
            def body(r, carry):
                bias_copy(a, r).start()
                return carry

            lax.fori_loop(1, lon_count, body, 0)

        for copy in own_copies:
            copy.wait()
        for copy in halo_copies[0]:
            copy.wait()

        grads = []
        db = None
        levels = [[load_level(which, z) for z in range(2)] for which in range(2)]
        for c in range(2):
            t = jnp.concatenate([nn(pc[c], levels[0][z]) for z in range(2)], axis=0)
            ct = jnp.concatenate([nn(pc[c], levels[1][z]) for z in range(2)], axis=0).astype(BF)
            grad, dscores = segment(t, ct, bt0[...], sel[...], mask[...])
            grads.append(grad)
            db = dscores if db is None else db + dscores
        for tile in range(OWNERS // 2):
            top = db[0:72, 128 * tile : 128 * tile + 128]
            bottom = db[72:144, 128 * tile : 128 * tile + 128]
            sb0[2 * tile] = jnp.where(lane, top, pltpu.roll(bottom, 64, 1)).astype(BF)
            sb0[2 * tile + 1] = jnp.where(lane, pltpu.roll(top, 64, 1), bottom).astype(BF)
        send_bias(0)
        for z in range(2):
            store_level(z, [grad[72 * z : 72 * z + 72] for grad in grads])
        grad_copies = send_grads(0)

        for g in (1, 2):
            for copy in halo_copies[g]:
                copy.wait()
        for s in range(2):
            tokens_here, cot_here = load_level(0, 2 + s), load_level(1, 2 + s)
            grads = []
            db = None
            for c in range(2):
                t = nn(pc[c], tokens_here)
                ct = nn(pc[c], cot_here).astype(BF)
                grad, dscores = segment(
                    t, ct, bt1[s], sel[0:72, 0 : LANES // 2], mask[:, 0 : LANES // 2]
                )
                grads.append(grad)
                db = dscores if db is None else db + dscores
            for tile in range(OWNERS // 4):
                part = db[:, 128 * tile : 128 * tile + 128]
                top, bottom = part[0:40], part[32:72]
                owner = OWNERS // 2 * s + 2 * tile
                sb1[owner] = jnp.where(lane, top, pltpu.roll(bottom, 64, 1)).astype(BF)
                sb1[owner + 1] = jnp.where(lane, pltpu.roll(top, 64, 1), bottom).astype(BF)
            store_level(2 + s, grads)
        send_bias(1)
        grad_copies += send_grads(1)

        for copy in grad_copies:
            copy.wait()
        for src, z, count in GROUPS:
            for i in range(count):
                out_ref[src + i, 0:3, 1:3] = rl[z + i, :, 1:3]
                out_ref[src + i, 0:3, 0] = rl[z + i, :, 0] + rd[z + i]
                out_ref[src + i, 3:6, 1:3] = ext[z + i, 0:3, 1:3]
                out_ref[src + i, 3:6, 0] = ext[z + i, 0:3, 0] + rc[z + i]

        def collect(r, carry):
            for a in range(2):
                bias_copy(a, r).wait()
            return carry[0] + rb0[r].astype(F32), carry[1] + rb1[r].astype(F32)

        sum0, sum1 = lax.fori_loop(
            1, lon_count, collect, (sb0[lon].astype(F32), sb1[lon].astype(F32))
        )
        first = jnp.concatenate([sum0, pltpu.roll(sum0, 64, 1)], axis=0)
        second = jnp.concatenate([pltpu.roll(sum1, 64, 1), sum1[8:40]], axis=0)
        early = lon < OWNERS // 2
        second = jnp.concatenate(
            [jnp.where(early, second, 0.0), jnp.where(early, 0.0, second)], axis=0
        )
        both = jnp.where(lane, first, second).T
        for a in range(2):
            for h in range(HEADS):
                bout_ref[a, h] = both[64 * a + 9 * h : 64 * a + 9 * h + 9]

    return kernel


def make_local(lat_count, lon_count):
    def local(tokens, cotangent, norm_gain, inproj_weight, outproj_weight, bias):
        any_spec = pl.BlockSpec(memory_space=pl.ANY)
        vmem = pl.BlockSpec(memory_space=pltpu.VMEM)
        dma = pltpu.SemaphoreType.DMA
        grad, bias_grad = pl.pallas_call(
            make_kernel(lat_count, lon_count),
            out_shape=(
                jax.ShapeDtypeStruct((4, 6, 3, 8, C), BF),
                jax.ShapeDtypeStruct((2, HEADS, 9, 144), F32),
            ),
            in_specs=[any_spec, any_spec, vmem, vmem, vmem, any_spec],
            out_specs=(vmem, vmem),
            scratch_shapes=[
                pltpu.VMEM((2, 4, 6, 4, 8, C), BF),
                pltpu.VMEM((2, 864, 144), F32),
                pltpu.VMEM((144, LANES), F32),
                pltpu.VMEM((2, 72, LANES // 2), F32),
                pltpu.VMEM((144, LANES), BF),
                pltpu.VMEM((C, LANES), BF),
                pltpu.VMEM((2, 72, 192), BF),
                pltpu.VMEM((2, 192, 72), BF),
                pltpu.VMEM((C, C), BF),
                pltpu.VMEM((C, C), BF),
                pltpu.VMEM((C, C), BF),
                pltpu.VMEM((C, C), BF),
                pltpu.VMEM((C, C), BF),
                pltpu.VMEM((4, 6, 4, 8, C), BF),
                pltpu.VMEM((OWNERS, 72, 128), BF),
                pltpu.VMEM((OWNERS, 40, 128), BF),
                pltpu.VMEM((OWNERS, 72, 128), BF),
                pltpu.VMEM((OWNERS, 40, 128), BF),
                pltpu.VMEM((4, 3, 3, 8, C), BF),
                pltpu.VMEM((4, 3, 8, C), BF),
                pltpu.VMEM((4, 3, 8, C), BF),
                dma((2,)),
                dma((2, 3)),
                dma((2, 3, 3)),
                dma((2, 3, 3)),
                dma((2, OWNERS)),
                dma((2, OWNERS)),
                dma((2, 3)),
                dma((2, 3)),
            ],
            compiler_params=pltpu.CompilerParams(collective_id=0, has_side_effects=True),
        )(
            tokens.reshape(4, 6, 3, 8, C),
            cotangent.reshape(4, 6, 3, 8, C),
            norm_gain.reshape(1, C),
            inproj_weight,
            outproj_weight,
            bias.reshape(2, 864, 144),
        )
        return grad.reshape(4, 6, 24, C), bias_grad.reshape(2, 1, HEADS, 9, 144)

    return local


def solution(mesh):
    placed = (
        P(None, "lat", "lon", None),
        P(None, "lat", "lon", None),
        P(),
        P(),
        P(),
        P(None, "lat", None, None, None),
    )
    return jax.shard_map(
        make_local(mesh.shape["lat"], mesh.shape["lon"]),
        mesh=mesh,
        in_specs=placed,
        out_specs=(P(None, "lat", "lon", None), P(None, "lat", None, "lon", None)),
        check_vma=False,
    )
```

```python
import jax
import jax.numpy as jnp
from jax import lax
from jax.experimental import pallas as pl
from jax.experimental.pallas import tpu as pltpu
from jax.sharding import PartitionSpec as P

EPS = 1e-05
HEADS = 6
C = 192
LOG2E = 1.4426950408889634
LN2 = 0.6931471805599453
SCALE = 32 ** (-0.5)
BF = jnp.bfloat16
F32 = jnp.float32
OWNERS = 16
HALF = 512
GROUPS = ((1, 0, 2), (3, 2, 1), (0, 3, 1))
MESH = pl.DeviceIdType.MESH


def nn(a, b):
    return lax.dot_general(a, b, (((1,), (0,)), ((), ())), preferred_element_type=F32)


def nt(a, b):
    return lax.dot_general(a, b, (((1,), (1,)), ((), ())), preferred_element_type=F32)


def tn(a, b):
    return lax.dot_general(a, b, (((0,), (0,)), ((), ())), preferred_element_type=F32)


def iota(shape, dim):
    return lax.broadcasted_iota(jnp.int32, shape, dim)


def one_hot(cond):
    return jnp.where(cond, 1.0, 0.0).astype(BF)


def lane_head():
    return ((iota((1, HALF), 1) & 63) * 57) >> 9


def lane_query():
    lane = iota((1, HALF), 1)
    return 9 * (lane >> 6) + (lane & 63) - 9 * lane_head()


def make_kernel(lat_count, lon_count):
    def kernel(
        tok, cot, gain_hbm, win_hbm, wout_hbm, bias_ref, rb0, rb1, gfull, edge,
        x, bias_v, bt0, bt1, perm, permb, choose, mask, pcs, pct,
        gain_ref, win_ref, wout_ref, wq, wk, wv, wqt, wkt,
        normed, standard, inverse, qbd, ubd, keys, vals, keyt, gq, gk, gv, ext, sb0, sb1,
        in_sem, own_sem, hs_sem, hr_sem, bs_sem, br_sem, gs_sem, gr_sem, keep_sem,
    ):
        lat = lax.axis_index("lat")
        lon = lax.axis_index("lon")
        half_count = lon_count // 2
        own_half = lon // half_count
        place = lax.rem(lon, half_count)
        other_half = 1 - own_half
        lat_next = lax.rem(lat + 1, lat_count)
        lat_prev = lax.rem(lat + lat_count - 1, lat_count)
        lon_next = lax.rem(lon + 1, lon_count)
        lon_prev = lax.rem(lon + lon_count - 1, lon_count)

        barrier = pltpu.get_barrier_semaphore()

        def greet(r, carry):
            pl.semaphore_signal(
                barrier, inc=1, device_id=(lat, lax.rem(lon + r, lon_count)), device_id_type=MESH
            )
            return carry

        for there in ((lat_prev, lon), (lat_next, lon), (lat_prev, lon_prev), (lat_next, lon_next)):
            pl.semaphore_signal(barrier, inc=1, device_id=there, device_id_type=MESH)
        lax.fori_loop(1, lon_count, greet, 0)

        own_copies = [[], [], []]
        for g, (src, z, count) in enumerate(GROUPS):
            for which, ref in enumerate((tok, cot)):
                copy = pltpu.make_async_copy(
                    ref.at[src : src + count, 3:6],
                    x.at[which, z : z + count, 0:3, 0:3],
                    own_sem.at[which, g],
                )
                copy.start()
                own_copies[g].append(copy)
        in_copies = [
            pltpu.make_async_copy(source, target, in_sem.at[i])
            for i, (source, target) in enumerate(
                (
                    (bias_ref.at[0], bias_v.at[0]),
                    (bias_ref.at[1], bias_v.at[1]),
                    (win_hbm, win_ref),
                    (wout_hbm, wout_ref),
                    (gain_hbm, gain_ref),
                )
            )
        ]
        for copy in in_copies:
            copy.start()

        pl.semaphore_wait(barrier, lon_count - 1 + 4)

        halo_copies = [[], [], []]
        for g, (src, z, count) in enumerate(GROUPS):
            for which, ref in enumerate((tok, cot)):
                for kind, (source, target, there) in enumerate(
                    (
                        (ref.at[src : src + count, 0:3, 0], x.at[which, z : z + count, 3:6, 3], (lat_prev, lon_prev)),
                        (ref.at[src : src + count, 3:6, 0], x.at[which, z : z + count, 0:3, 3], (lat, lon_prev)),
                        (ref.at[src : src + count, 0:3], x.at[which, z : z + count, 3:6, 0:3], (lat_prev, lon)),
                    )
                ):
                    copy = pltpu.make_async_remote_copy(
                        src_ref=source,
                        dst_ref=target,
                        send_sem=hs_sem.at[which, kind, g],
                        recv_sem=hr_sem.at[which, kind, g],
                        device_id=there,
                        device_id_type=MESH,
                    )
                    copy.start()
                    halo_copies[g].append(copy)

        heads, queries = lane_head(), lane_query()
        perm[...] = one_hot(iota((128 * HEADS, HALF), 0) == 128 * heads + queries)
        permb[...] = one_hot(iota((72 * HEADS, HALF), 0) == 72 * heads + queries)
        choose[...] = one_hot((iota((72, HALF), 0) == queries) & (heads < HEADS))
        mask[...] = one_hot((iota((C, HALF), 0) >> 5) == heads)
        for c in range(2):
            p = iota((72, 192), 0)
            row = (p * 43) >> 9
            pcs[c] = one_hot(iota((72, 192), 1) == 32 * row + p - 12 * row + 6 + 12 * c)
            p = iota((192, 72), 1)
            row = (p * 43) >> 9
            pct[c] = one_hot(iota((192, 72), 0) == 32 * row + p - 12 * row + 6 + 12 * c)
        for copy in in_copies:
            copy.wait()
        wq[...] = win_ref[:, 0:192]
        wk[...] = win_ref[:, 192:384]
        wv[...] = win_ref[:, 384:576]
        wqt[...] = wq[...].astype(F32).T.astype(BF)
        wkt[...] = wk[...].astype(F32).T.astype(BF)

        is_last = jnp.where(lat == lat_count - 1, -1e30, 0.0).astype(F32)
        query_late = queries >= 36

        def penalty(rows):
            return jnp.where((lax.rem(iota((rows, 1), 0), 72) >= 36) != query_late, is_last, 0.0)

        for a in range(2):
            for s in range(2):
                b = LOG2E * jnp.concatenate(
                    [bias_v[a, 144 * h + 72 * s : 144 * h + 72 * s + 72, :] for h in range(HEADS)], axis=0
                )
                high = b.astype(BF)
                low = (b - high.astype(F32)).astype(BF)
                moved = tn(high, permb[...]) + tn(low, permb[...])
                if a == 0:
                    bt0[s] = moved + penalty(144)
                else:
                    bt1[s] = moved[72 * s : 72 * s + 72] + penalty(72)

        gain = gain_ref[...]
        lane = iota((1, 128), 1) < 64
        blank = jnp.zeros((56, C), F32)

        def prepare(a):
            for l in range(2):
                t = nn(pcs[...].reshape(144, 192), x[0, 2 * a + l].reshape(192, C))
                centred = t - jnp.sum(t, axis=-1, keepdims=True) * (1.0 / C)
                inv = lax.rsqrt(jnp.sum(centred * centred, axis=-1, keepdims=True) * (1.0 / C) + EPS)
                unit = centred * inv
                inverse[l] = inv
                standard[l] = unit
                normed[l] = unit * gain
            compact = []
            for l in range(2):
                ct = nn(pcs[...].reshape(144, 192), x[1, 2 * a + l].reshape(192, C))
                for c in range(2):
                    rows = slice(72 * c, 72 * c + 72)
                    padded = jnp.concatenate([normed[l, rows], blank], axis=0).astype(BF)
                    qt = (nt(wqt[...], padded) * (SCALE * LOG2E)).astype(BF)
                    ut = nt(wout_ref[...], jnp.concatenate([ct[rows], blank], axis=0).astype(BF)).astype(BF)
                    for side in (qt, ut):
                        compact.append(
                            jnp.concatenate([side[32 * h : 32 * h + 32] for h in range(HEADS)], axis=1)
                        )
            wide = nn(jnp.concatenate(compact, axis=0), perm[...]).astype(BF)
            for l in range(2):
                for c in range(2):
                    at = 64 * (2 * l + c)
                    qbd[l, c] = jnp.concatenate([wide[at : at + 32]] * HEADS, axis=0) * mask[...]
                    ubd[l, c] = jnp.concatenate([wide[at + 32 : at + 64]] * HEADS, axis=0) * mask[...]

        def block(k, v, kt, s, c, biast):
            q, u = qbd[s, c], ubd[s, c]
            e = jnp.exp2(nn(k, q) + biast)
            probs = e * (1.0 / jnp.sum(e, axis=0, keepdims=True))
            weighted = probs * nn(v, u)
            dscores = weighted - probs * jnp.sum(weighted, axis=0, keepdims=True)
            low = dscores.astype(BF)
            dv = nt(probs.astype(BF), u)
            dk = nt(low, q) * LN2
            gq[s, c] = nt(choose[...], nn(kt, low).astype(BF) * mask[...])
            return dk, dv, dscores

        def finish(a):
            dq, dk, dv = (ref[...].reshape(288, C).astype(BF) for ref in (gq, gk, gv))
            scaled = (nt(dq, wq[...]) + nt(dk, wk[...]) + nt(dv, wv[...])) * gain
            for l in range(2):
                part = scaled[144 * l : 144 * l + 144]
                unit = standard[l]
                grad = inverse[l] * (
                    part
                    - jnp.sum(part, axis=-1, keepdims=True) * (1.0 / C)
                    - unit * (jnp.sum(part * unit, axis=-1, keepdims=True) * (1.0 / C))
                )
                full = nn(pct[0], grad[0:72].astype(BF)) + nn(pct[1], grad[72:144].astype(BF))
                ext[(2 * a + l + 1) % 4] = full.reshape(6, 4, 8, C).astype(BF)

        def send_grads(groups):
            copies = []
            for g in groups:
                level, _, count = GROUPS[g]
                span = pl.ds(level, count)
                for kind, (source, target, there) in enumerate(
                    (
                        (ext.at[span, 3:6, 3], edge.at[span, 0:3], (lat_next, lon_next)),
                        (ext.at[span, 0:3, 3], edge.at[span, 3:6], (lat, lon_next)),
                        (ext.at[span, 3:6, 0:3], gfull.at[span, 0:3], (lat_next, lon)),
                    )
                ):
                    copies.append(
                        pltpu.make_async_remote_copy(
                            src_ref=source,
                            dst_ref=target,
                            send_sem=gs_sem.at[g, kind],
                            recv_sem=gr_sem.at[g, kind],
                            device_id=there,
                            device_id_type=MESH,
                        )
                    )
                copies.append(
                    pltpu.make_async_copy(
                        ext.at[span, 0:3, 0:3], gfull.at[span, 3:6], keep_sem.at[g]
                    )
                )
            for copy in copies:
                copy.start()
            return copies

        def bias_copy(a, slot):
            half = jnp.where(slot >= half_count, other_half, own_half)
            there = half_count * half + lax.rem(place + slot, half_count)
            source, target = ((sb0, rb0), (sb1, rb1))[a]
            return pltpu.make_async_remote_copy(
                src_ref=source.at[there],
                dst_ref=target.at[slot],
                send_sem=bs_sem.at[a, slot],
                recv_sem=br_sem.at[a, slot],
                device_id=(lat, there),
                device_id_type=MESH,
            )

        def keep_copy(a):
            source, target = ((sb0, rb0), (sb1, rb1))[a]
            return pltpu.make_async_copy(source.at[lon], target.at[0], keep_sem.at[3 + a])

        def send_bias(a, i):
            def body(slot, carry):
                bias_copy(a, slot).start()
                return carry

            if i == 0:
                lax.fori_loop(half_count, lon_count, body, 0)
            else:
                lax.fori_loop(1, half_count, body, 0)
                keep_copy(a).start()

        def arrived(g):
            for copy in own_copies[g] + halo_copies[g]:
                copy.wait()

        arrived(0)
        prepare(0)
        for c in range(2):
            whole = jnp.concatenate([normed[l, 72 * c : 72 * c + 72] for l in range(2)], axis=0).astype(BF)
            keys[c] = nn(whole, wk[...]).astype(BF)
            vals[c] = nn(whole, wv[...]).astype(BF)
            keyt[c] = (nt(wkt[...], whole) * SCALE).astype(BF)
        totals = [None, None]
        for i, s in enumerate((other_half, own_half)):
            db = None
            for c in range(2):
                dk, dv, dscores = block(keys[c], vals[c], keyt[c], s, c, bt0[s])
                db = dscores if db is None else db + dscores
                totals[c] = (dk, dv) if i == 0 else (totals[c][0] + dk, totals[c][1] + dv)
            for tile in range(4):
                top = db[0:72, 128 * tile : 128 * tile + 128]
                bottom = db[72:144, 128 * tile : 128 * tile + 128]
                owner = half_count * s + 2 * tile
                sb0[owner] = jnp.where(lane, top, pltpu.roll(bottom, 64, 1)).astype(BF)
                sb0[owner + 1] = jnp.where(lane, pltpu.roll(top, 64, 1), bottom).astype(BF)
            send_bias(0, i)
        for c in range(2):
            for l in range(2):
                gk[l, c] = totals[c][0][72 * l : 72 * l + 72]
                gv[l, c] = totals[c][1][72 * l : 72 * l + 72]
        finish(0)
        grad_copies = send_grads((0,))

        arrived(1)
        arrived(2)
        prepare(1)
        for l in range(2):
            for c in range(2):
                part = normed[l, 72 * c : 72 * c + 72].astype(BF)
                keys[2 + 2 * l + c, 0:72] = nn(part, wk[...]).astype(BF)
                vals[2 + 2 * l + c, 0:72] = nn(part, wv[...]).astype(BF)
                keyt[2 + 2 * l + c, :, 0:72] = (nt(wkt[...], part) * SCALE).astype(BF)
        for i, s in enumerate((other_half, own_half)):
            db = None
            for c in range(2):
                at = 2 + 2 * s + c
                dk, dv, dscores = block(
                    keys[at, 0:72], vals[at, 0:72], keyt[at, :, 0:72], s, c, bt1[s]
                )
                gk[s, c] = dk
                gv[s, c] = dv
                db = dscores if db is None else db + dscores
            for tile in range(4):
                part = db[:, 128 * tile : 128 * tile + 128]
                top, bottom = part[0:40], part[32:72]
                owner = half_count * s + 2 * tile
                sb1[owner] = jnp.where(lane, top, pltpu.roll(bottom, 64, 1)).astype(BF)
                sb1[owner + 1] = jnp.where(lane, pltpu.roll(top, 64, 1), bottom).astype(BF)
            send_bias(1, i)
        finish(1)
        grad_copies += send_grads((1, 2))

        for copy in grad_copies:
            copy.wait()
        for a in range(2):
            keep_copy(a).wait()

        def collect(slot, carry):
            for a in range(2):
                bias_copy(a, slot).wait()
            return carry

        lax.fori_loop(1, lon_count, collect, 0)

    return kernel


def make_final(lon_count):
    def final(rb0, rb1, gfull, edge, out_ref, bout_ref):
        lane = iota((1, 128), 1) < 64
        out_ref[:, :, 1:3] = gfull[:, :, 1:3]
        out_ref[:, :, 0] = gfull[:, :, 0] + edge[...]
        sum0, sum1 = rb0[0].astype(F32), rb1[0].astype(F32)
        for slot in range(1, lon_count):
            sum0 += rb0[slot].astype(F32)
            sum1 += rb1[slot].astype(F32)
        first = jnp.concatenate([sum0, pltpu.roll(sum0, 64, 1)], axis=0)
        second = jnp.concatenate([pltpu.roll(sum1, 64, 1), sum1[8:40]], axis=0)
        early = lax.axis_index("lon") < lon_count // 2
        second = jnp.concatenate(
            [jnp.where(early, second, 0.0), jnp.where(early, 0.0, second)], axis=0
        )
        both = jnp.where(lane, first, second).T
        for a in range(2):
            for h in range(HEADS):
                for q in range(9):
                    at = 64 * a + 9 * h + q
                    bout_ref[a, h, q] = both[at : at + 1]

    return final


def make_local(lat_count, lon_count):
    def local(tokens, cotangent, norm_gain, inproj_weight, outproj_weight, bias):
        any_spec = pl.BlockSpec(memory_space=pl.ANY)
        vmem = pl.BlockSpec(memory_space=pltpu.VMEM)
        dma = pltpu.SemaphoreType.DMA
        parts = pl.pallas_call(
            make_kernel(lat_count, lon_count),
            out_shape=(
                jax.ShapeDtypeStruct((OWNERS, 72, 128), BF),
                jax.ShapeDtypeStruct((OWNERS, 40, 128), BF),
                jax.ShapeDtypeStruct((4, 6, 3, 8, C), BF),
                jax.ShapeDtypeStruct((4, 6, 8, C), BF),
            ),
            in_specs=[any_spec] * 6,
            out_specs=(any_spec,) * 4,
            scratch_shapes=[
                pltpu.VMEM((2, 4, 6, 4, 8, C), BF),
                pltpu.VMEM((2, 864, 144), F32),
                pltpu.VMEM((2, 144, HALF), F32),
                pltpu.VMEM((2, 72, HALF), F32),
                pltpu.VMEM((128 * HEADS, HALF), BF),
                pltpu.VMEM((72 * HEADS, HALF), BF),
                pltpu.VMEM((72, HALF), BF),
                pltpu.VMEM((C, HALF), BF),
                pltpu.VMEM((2, 72, 192), BF),
                pltpu.VMEM((2, 192, 72), BF),
                pltpu.VMEM((1, C), F32),
                pltpu.VMEM((C, 3 * C), BF),
                pltpu.VMEM((C, C), BF),
            ]
            + [pltpu.VMEM((C, C), BF)] * 5
            + [
                pltpu.VMEM((2, 144, C), F32),
                pltpu.VMEM((2, 144, C), F32),
                pltpu.VMEM((2, 144, 1), F32),
                pltpu.VMEM((2, 2, C, HALF), BF),
                pltpu.VMEM((2, 2, C, HALF), BF),
                pltpu.VMEM((6, 144, C), BF),
                pltpu.VMEM((6, 144, C), BF),
                pltpu.VMEM((6, C, 144), BF),
                pltpu.VMEM((2, 2, 72, C), F32),
                pltpu.VMEM((2, 2, 72, C), F32),
                pltpu.VMEM((2, 2, 72, C), F32),
                pltpu.VMEM((4, 6, 4, 8, C), BF),
                pltpu.VMEM((OWNERS, 72, 128), BF),
                pltpu.VMEM((OWNERS, 40, 128), BF),
                dma((5,)),
                dma((2, 3)),
                dma((2, 3, 3)),
                dma((2, 3, 3)),
                dma((2, OWNERS)),
                dma((2, OWNERS)),
                dma((3, 3)),
                dma((3, 3)),
                dma((5,)),
            ],
            compiler_params=pltpu.CompilerParams(collective_id=0, has_side_effects=True),
        )(
            tokens.reshape(4, 6, 3, 8, C),
            cotangent.reshape(4, 6, 3, 8, C),
            norm_gain.reshape(1, C),
            inproj_weight,
            outproj_weight,
            bias.reshape(2, 864, 144),
        )
        grad, bias_grad = pl.pallas_call(
            make_final(lon_count),
            out_shape=(
                jax.ShapeDtypeStruct((4, 6, 3, 8, C), BF),
                jax.ShapeDtypeStruct((2, HEADS, 9, 1, 144), F32),
            ),
            in_specs=[vmem] * 4,
            out_specs=(vmem, vmem),
        )(*parts)
        return grad.reshape(4, 6, 24, C), bias_grad.reshape(2, 1, HEADS, 9, 144)

    return local


def solution(mesh):
    placed = (
        P(None, "lat", "lon", None),
        P(None, "lat", "lon", None),
        P(),
        P(),
        P(),
        P(None, "lat", None, None, None),
    )
    return jax.shard_map(
        make_local(mesh.shape["lat"], mesh.shape["lon"]),
        mesh=mesh,
        in_specs=placed,
        out_specs=(P(None, "lat", "lon", None), P(None, "lat", None, "lon", None)),
        check_vma=False,
    )
```

```python
import jax
import jax.numpy as jnp
from jax import lax
from jax.experimental import pallas as pl
from jax.experimental.pallas import tpu as pltpu
from jax.sharding import PartitionSpec as P

EPS = 1e-05
HEADS = 6
C = 192
LOG2E = 1.4426950408889634
LN2 = 0.6931471805599453
SCALE = 32 ** (-0.5)
BF = jnp.bfloat16
F32 = jnp.float32
OWNERS = 16
HALF = 512
GROUPS = ((1, 0, 2), (3, 2, 1), (0, 3, 1))
MESH = pl.DeviceIdType.MESH


def nn(a, b):
    return lax.dot_general(a, b, (((1,), (0,)), ((), ())), preferred_element_type=F32)


def nt(a, b):
    return lax.dot_general(a, b, (((1,), (1,)), ((), ())), preferred_element_type=F32)


def tn(a, b):
    return lax.dot_general(a, b, (((0,), (0,)), ((), ())), preferred_element_type=F32)


def iota(shape, dim):
    return lax.broadcasted_iota(jnp.int32, shape, dim)


def one_hot(cond):
    return jnp.where(cond, 1.0, 0.0).astype(BF)


def lane_head():
    return ((iota((1, HALF), 1) & 63) * 57) >> 9


def lane_query():
    lane = iota((1, HALF), 1)
    return 9 * (lane >> 6) + (lane & 63) - 9 * lane_head()


def make_kernel(lat_count, lon_count):
    def kernel(
        tok, cot, gain_hbm, win_hbm, wout_hbm, bias_ref, rb0, rb1, gfull, edge,
        x, bias_v, bt0, bt1, perm, permb, choose, mask, pcs, pct,
        gain_ref, win_ref, wout_ref, wq, wk, wv, wqkt,
        standard, inverse, qbd, ubd, keys, vals, keyt, gq, gk, gv, ext, sb0, sb1,
        in_sem, own_sem, hs_sem, hr_sem, bs_sem, br_sem, gs_sem, gr_sem, keep_sem,
    ):
        lat = lax.axis_index("lat")
        lon = lax.axis_index("lon")
        half_count = lon_count // 2
        own_half = lon // half_count
        place = lax.rem(lon, half_count)
        other_half = 1 - own_half
        lat_next = lax.rem(lat + 1, lat_count)
        lat_prev = lax.rem(lat + lat_count - 1, lat_count)
        lon_next = lax.rem(lon + 1, lon_count)
        lon_prev = lax.rem(lon + lon_count - 1, lon_count)

        barrier = pltpu.get_barrier_semaphore()

        def greet(r, carry):
            pl.semaphore_signal(
                barrier, inc=1, device_id=(lat, lax.rem(lon + r, lon_count)), device_id_type=MESH
            )
            return carry

        for there in ((lat_prev, lon), (lat_next, lon), (lat_prev, lon_prev), (lat_next, lon_next)):
            pl.semaphore_signal(barrier, inc=1, device_id=there, device_id_type=MESH)
        lax.fori_loop(1, lon_count, greet, 0)

        own_copies = [[], [], []]
        for g, (src, z, count) in enumerate(GROUPS):
            for which, ref in enumerate((tok, cot)):
                copy = pltpu.make_async_copy(
                    ref.at[src : src + count, 3:6],
                    x.at[which, z : z + count, 0:3, 0:3],
                    own_sem.at[which, g],
                )
                copy.start()
                own_copies[g].append(copy)
        in_copies = [
            pltpu.make_async_copy(source, target, in_sem.at[i])
            for i, (source, target) in enumerate(
                (
                    (bias_ref.at[0], bias_v.at[0]),
                    (bias_ref.at[1], bias_v.at[1]),
                    (win_hbm, win_ref),
                    (wout_hbm, wout_ref),
                    (gain_hbm, gain_ref),
                )
            )
        ]
        for copy in in_copies:
            copy.start()

        pl.semaphore_wait(barrier, lon_count - 1 + 4)

        halo_copies = [[], [], []]
        for g, (src, z, count) in enumerate(GROUPS):
            for which, ref in enumerate((tok, cot)):
                for kind, (source, target, there) in enumerate(
                    (
                        (ref.at[src : src + count, 0:3, 0], x.at[which, z : z + count, 3:6, 3], (lat_prev, lon_prev)),
                        (ref.at[src : src + count, 3:6, 0], x.at[which, z : z + count, 0:3, 3], (lat, lon_prev)),
                        (ref.at[src : src + count, 0:3], x.at[which, z : z + count, 3:6, 0:3], (lat_prev, lon)),
                    )
                ):
                    copy = pltpu.make_async_remote_copy(
                        src_ref=source,
                        dst_ref=target,
                        send_sem=hs_sem.at[which, kind, g],
                        recv_sem=hr_sem.at[which, kind, g],
                        device_id=there,
                        device_id_type=MESH,
                    )
                    copy.start()
                    halo_copies[g].append(copy)

        heads, queries = lane_head(), lane_query()
        perm[...] = one_hot(iota((128 * HEADS, HALF), 0) == 128 * heads + queries)
        permb[...] = one_hot(iota((72 * HEADS, HALF), 0) == 72 * heads + queries)
        choose[...] = one_hot((iota((72, HALF), 0) == queries) & (heads < HEADS))
        mask[...] = one_hot((iota((C, HALF), 0) >> 5) == heads)
        def grid_place(token):
            c = (token >= 72).astype(jnp.int32)
            inside = token - 72 * c
            row = (inside * 43) >> 9
            return 32 * row + inside - 12 * row + 6 + 12 * c

        pcs[...] = one_hot(iota((144, 192), 1) == grid_place(iota((144, 192), 0)))
        pct[...] = one_hot(iota((192, 144), 0) == grid_place(iota((192, 144), 1)))
        for copy in in_copies:
            copy.wait()
        wq[...] = win_ref[:, 0:192]
        wk[...] = win_ref[:, 192:384]
        wv[...] = win_ref[:, 384:576]
        wqkt[0:192] = wq[...].astype(F32).T.astype(BF)
        wqkt[192:384] = wk[...].astype(F32).T.astype(BF)

        is_last = jnp.where(lat == lat_count - 1, -1e30, 0.0).astype(F32)
        query_late = queries >= 36

        def penalty(rows):
            return jnp.where((lax.rem(iota((rows, 1), 0), 72) >= 36) != query_late, is_last, 0.0)

        for a in range(2):
            for s in range(2):
                b = LOG2E * jnp.concatenate(
                    [bias_v[a, 144 * h + 72 * s : 144 * h + 72 * s + 72, :] for h in range(HEADS)], axis=0
                )
                high = b.astype(BF)
                low = (b - high.astype(F32)).astype(BF)
                moved = tn(high, permb[...]) + tn(low, permb[...])
                if a == 0:
                    bt0[s] = moved + penalty(144)
                else:
                    bt1[s] = moved[72 * s : 72 * s + 72] + penalty(72)

        gain = gain_ref[...]
        lane = iota((1, 128), 1) < 64
        blank = jnp.zeros((56, C), F32)

        def pad_pair(v):
            return jnp.concatenate([v[0:72], blank, v[72:144], blank], axis=0).astype(BF)

        def compact(sides):
            return jnp.concatenate(
                [
                    jnp.concatenate(
                        [side[32 * h : 32 * h + 32, 128 * c : 128 * c + 128] for h in range(HEADS)], axis=1
                    )
                    for side in sides
                    for c in range(2)
                ],
                axis=0,
            )

        def expand(target, wide):
            for l in range(2):
                for c in range(2):
                    at = 32 * (2 * l + c)
                    target[l, c] = jnp.concatenate([wide[at : at + 32]] * HEADS, axis=0) * mask[...]

        def prepare(a):
            ts = [nn(pcs[...], x[0, 2 * a + l].reshape(192, C)) for l in range(2)]
            cts = [nn(pcs[...], x[1, 2 * a + l].reshape(192, C)) for l in range(2)]
            yield
            uts = [nt(wout_ref[...], pad_pair(cts[l])).astype(BF) for l in range(2)]
            plain = []
            for l in range(2):
                centred = ts[l] - jnp.sum(ts[l], axis=-1, keepdims=True) * (1.0 / C)
                inv = lax.rsqrt(jnp.sum(centred * centred, axis=-1, keepdims=True) * (1.0 / C) + EPS)
                unit = centred * inv
                inverse[a, l] = inv
                standard[a, l] = unit
                plain.append(unit * gain)
            yield
            expand(ubd.at[a], nn(compact(uts), perm[...]).astype(BF))
            yield
            qts = []
            for l in range(2):
                projected = nt(wqkt[...] if a else wqkt[0:192], pad_pair(plain[l]))
                qts.append((projected[0:192] * (SCALE * LOG2E)).astype(BF))
                if a:
                    for c in range(2):
                        keyt[2 + 2 * l + c, :, 0:72] = (
                            projected[192:384, 128 * c : 128 * c + 72] * SCALE
                        ).astype(BF)
            yield
            together = jnp.concatenate(plain, axis=0).astype(BF)
            for target, weight in ((keys, wk), (vals, wv)):
                rows = nn(together, weight[...])
                for c in range(2):
                    if a:
                        for l in range(2):
                            at = 144 * l + 72 * c
                            target[2 + 2 * l + c, 0:72] = rows[at : at + 72].astype(BF)
                    else:
                        target[c] = jnp.concatenate(
                            [rows[72 * c : 72 * c + 72], rows[144 + 72 * c : 216 + 72 * c]], axis=0
                        ).astype(BF)
            if not a:
                for c in range(2):
                    whole = jnp.concatenate([v[72 * c : 72 * c + 72] for v in plain], axis=0).astype(BF)
                    keyt[c] = (nt(wqkt[192:384], whole) * SCALE).astype(BF)
            yield
            expand(qbd.at[a], nn(compact(qts), perm[...]).astype(BF))
            yield

        sums = {}
        parts = {}

        def block(a, s, c):
            if a:
                at = 2 + 2 * s + c
                k, v, kt, biast = keys[at, 0:72], vals[at, 0:72], keyt[at, :, 0:72], bt1[s]
            else:
                k, v, kt, biast = keys[c], vals[c], keyt[c], bt0[s]
            scores = nn(k, qbd[a, s, c])
            dprobs = nn(v, ubd[a, s, c])
            yield
            e = jnp.exp2(scores + biast)
            probs = e * (1.0 / jnp.sum(e, axis=0, keepdims=True))
            weighted = probs * dprobs
            dscores = weighted - probs * jnp.sum(weighted, axis=0, keepdims=True)
            sums[a, s] = dscores if c == 0 else sums[a, s] + dscores
            low = dscores.astype(BF)
            dv = nt(probs.astype(BF), ubd[a, s, c])
            wide = nn(kt, low)
            dk = nt(low, qbd[a, s, c]) * LN2
            if a:
                gk[a, s, c] = dk
                gv[a, s, c] = dv
            elif s == 0:
                parts[c] = (dk, dv)
            else:
                for target, total in ((gk, parts[c][0] + dk), (gv, parts[c][1] + dv)):
                    for l in range(2):
                        target[a, l, c] = total[72 * l : 72 * l + 72]
            yield
            gq[a, s, c] = nt(choose[...], wide.astype(BF) * mask[...])
            yield

        def pack(a, s):
            for tile in range(4):
                part = sums[a, s][:, 128 * tile : 128 * tile + 128]
                target, top, bottom = (sb1, part[0:40], part[32:72]) if a else (sb0, part[0:72], part[72:144])
                owner = 8 * s + 2 * tile
                target[owner] = jnp.where(lane, top, pltpu.roll(bottom, 64, 1)).astype(BF)
                target[owner + 1] = jnp.where(lane, pltpu.roll(top, 64, 1), bottom).astype(BF)

        def finish(a):
            dq, dk, dv = (ref[a].reshape(288, C).astype(BF) for ref in (gq, gk, gv))
            scaled = (nt(dq, wq[...]) + nt(dk, wk[...]) + nt(dv, wv[...])) * gain
            yield
            for l in range(2):
                part = scaled[144 * l : 144 * l + 144]
                unit = standard[a, l]
                grad = inverse[a, l] * (
                    part
                    - jnp.sum(part, axis=-1, keepdims=True) * (1.0 / C)
                    - unit * (jnp.sum(part * unit, axis=-1, keepdims=True) * (1.0 / C))
                )
                ext[(2 * a + l + 1) % 4] = nn(pct[...], grad.astype(BF)).reshape(6, 4, 8, C).astype(BF)
            yield

        def send_grads(groups):
            copies = []
            for g in groups:
                level, _, count = GROUPS[g]
                span = pl.ds(level, count)
                for kind, (source, target, there) in enumerate(
                    (
                        (ext.at[span, 3:6, 3], edge.at[span, 0:3], (lat_next, lon_next)),
                        (ext.at[span, 0:3, 3], edge.at[span, 3:6], (lat, lon_next)),
                        (ext.at[span, 3:6, 0:3], gfull.at[span, 0:3], (lat_next, lon)),
                    )
                ):
                    copies.append(
                        pltpu.make_async_remote_copy(
                            src_ref=source,
                            dst_ref=target,
                            send_sem=gs_sem.at[g, kind],
                            recv_sem=gr_sem.at[g, kind],
                            device_id=there,
                            device_id_type=MESH,
                        )
                    )
                copies.append(
                    pltpu.make_async_copy(
                        ext.at[span, 0:3, 0:3], gfull.at[span, 3:6], keep_sem.at[g]
                    )
                )
            for copy in copies:
                copy.start()
            return copies

        def bias_copy(a, slot):
            half = other_half if slot >= half_count else own_half
            there = half_count * half + ((place + slot) & (half_count - 1))
            source, target = ((sb0, rb0), (sb1, rb1))[a]
            return pltpu.make_async_remote_copy(
                src_ref=source.at[there],
                dst_ref=target.at[slot],
                send_sem=bs_sem.at[a, slot],
                recv_sem=br_sem.at[a, slot],
                device_id=(lat, there),
                device_id_type=MESH,
            )

        def keep_copy(a):
            source, target = ((sb0, rb0), (sb1, rb1))[a]
            return pltpu.make_async_copy(source.at[lon], target.at[0], keep_sem.at[3 + a])

        def send_bias(a):
            for slot in range(half_count, lon_count):
                bias_copy(a, slot).start()
            for slot in range(1, half_count):
                bias_copy(a, slot).start()
            keep_copy(a).start()

        def arrived(g):
            for copy in own_copies[g] + halo_copies[g]:
                copy.wait()

        def run(*pieces):
            for piece in pieces:
                next(piece)

        p0, p1, f0, f1 = prepare(0), prepare(1), finish(0), finish(1)
        b0, b1, b2, b3 = (block(0, s, c) for s in range(2) for c in range(2))
        b4, b5, b6, b7 = (block(1, s, c) for s in range(2) for c in range(2))
        arrived(0)
        run(*[p0] * 6)
        arrived(1)
        arrived(2)
        run(p1, b0, b1, p1, p1, b0, b2, p1, b1, b0, b3, p1, b1)
        pack(0, 0)
        run(p1, b2, b4, b2, b3, b5, b3)
        pack(0, 1)
        send_bias(0)
        run(f0, b4, b6, f0)
        grad_copies = send_grads((0,))
        run(b4, b5, b7, b5, b6, b6, b7, b7, f1, f1)
        grad_copies += send_grads((1, 2))
        pack(1, 0)
        pack(1, 1)
        send_bias(1)

        for copy in grad_copies:
            copy.wait()
        for a in range(2):
            keep_copy(a).wait()

        for a in range(2):
            for slot in range(1, lon_count):
                bias_copy(a, slot).wait()

    return kernel


def make_final(lon_count):
    def final(rb0, rb1, gfull, edge, out_ref, bout_ref):
        lane = iota((1, 128), 1) < 64
        out_ref[:, :, 1:3] = gfull[:, :, 1:3]
        out_ref[:, :, 0] = gfull[:, :, 0] + edge[...]
        sum0, sum1 = rb0[0].astype(F32), rb1[0].astype(F32)
        for slot in range(1, lon_count):
            sum0 += rb0[slot].astype(F32)
            sum1 += rb1[slot].astype(F32)
        first = jnp.concatenate([sum0, pltpu.roll(sum0, 64, 1)], axis=0)
        second = jnp.concatenate([pltpu.roll(sum1, 64, 1), sum1[8:40]], axis=0)
        early = lax.axis_index("lon") < lon_count // 2
        second = jnp.concatenate(
            [jnp.where(early, second, 0.0), jnp.where(early, 0.0, second)], axis=0
        )
        both = jnp.where(lane, first, second).T
        for a in range(2):
            for h in range(HEADS):
                for q in range(9):
                    at = 64 * a + 9 * h + q
                    bout_ref[a, h, q] = both[at : at + 1]

    return final


def make_local(lat_count, lon_count):
    def local(tokens, cotangent, norm_gain, inproj_weight, outproj_weight, bias):
        any_spec = pl.BlockSpec(memory_space=pl.ANY)
        vmem = pl.BlockSpec(memory_space=pltpu.VMEM)
        dma = pltpu.SemaphoreType.DMA
        parts = pl.pallas_call(
            make_kernel(lat_count, lon_count),
            out_shape=(
                pltpu.VMEM((OWNERS, 72, 128), BF),
                pltpu.VMEM((OWNERS, 40, 128), BF),
                pltpu.VMEM((4, 6, 3, 8, C), BF),
                pltpu.VMEM((4, 6, 8, C), BF),
            ),
            in_specs=[any_spec] * 6,
            out_specs=(any_spec,) * 4,
            scratch_shapes=[
                pltpu.VMEM((2, 4, 6, 4, 8, C), BF),
                pltpu.VMEM((2, 864, 144), F32),
                pltpu.VMEM((2, 144, HALF), F32),
                pltpu.VMEM((2, 72, HALF), F32),
                pltpu.VMEM((128 * HEADS, HALF), BF),
                pltpu.VMEM((72 * HEADS, HALF), BF),
                pltpu.VMEM((72, HALF), BF),
                pltpu.VMEM((C, HALF), BF),
                pltpu.VMEM((144, 192), BF),
                pltpu.VMEM((192, 144), BF),
                pltpu.VMEM((1, C), F32),
                pltpu.VMEM((C, 3 * C), BF),
                pltpu.VMEM((C, C), BF),
            ]
            + [pltpu.VMEM((C, C), BF)] * 3
            + [
                pltpu.VMEM((2 * C, C), BF),
                pltpu.VMEM((2, 2, 144, C), F32),
                pltpu.VMEM((2, 2, 144, 1), F32),
                pltpu.VMEM((2, 2, 2, C, HALF), BF),
                pltpu.VMEM((2, 2, 2, C, HALF), BF),
                pltpu.VMEM((6, 144, C), BF),
                pltpu.VMEM((6, 144, C), BF),
                pltpu.VMEM((6, C, 144), BF),
                pltpu.VMEM((2, 2, 2, 72, C), F32),
                pltpu.VMEM((2, 2, 2, 72, C), F32),
                pltpu.VMEM((2, 2, 2, 72, C), F32),
                pltpu.VMEM((4, 6, 4, 8, C), BF),
                pltpu.VMEM((OWNERS, 72, 128), BF),
                pltpu.VMEM((OWNERS, 40, 128), BF),
                dma((5,)),
                dma((2, 3)),
                dma((2, 3, 3)),
                dma((2, 3, 3)),
                dma((2, OWNERS)),
                dma((2, OWNERS)),
                dma((3, 3)),
                dma((3, 3)),
                dma((5,)),
            ],
            compiler_params=pltpu.CompilerParams(collective_id=0, has_side_effects=True),
        )(
            tokens.reshape(4, 6, 3, 8, C),
            cotangent.reshape(4, 6, 3, 8, C),
            norm_gain.reshape(1, C),
            inproj_weight,
            outproj_weight,
            bias.reshape(2, 864, 144),
        )
        grad, bias_grad = pl.pallas_call(
            make_final(lon_count),
            out_shape=(
                jax.ShapeDtypeStruct((4, 6, 3, 8, C), BF),
                jax.ShapeDtypeStruct((2, HEADS, 9, 1, 144), F32),
            ),
            in_specs=[vmem] * 4,
            out_specs=(vmem, vmem),
            compiler_params=pltpu.CompilerParams(vmem_limit_bytes=8 * 1024 * 1024),
        )(*parts)
        return grad.reshape(4, 6, 24, C), bias_grad.reshape(2, 1, HEADS, 9, 144)

    return local


def solution(mesh):
    placed = (
        P(None, "lat", "lon", None),
        P(None, "lat", "lon", None),
        P(),
        P(),
        P(),
        P(None, "lat", None, None, None),
    )
    return jax.shard_map(
        make_local(mesh.shape["lat"], mesh.shape["lon"]),
        mesh=mesh,
        in_specs=placed,
        out_specs=(P(None, "lat", "lon", None), P(None, "lat", None, "lon", None)),
        check_vma=False,
    )
```

```python
import jax
import jax.numpy as jnp
from jax import lax
from jax.experimental import pallas as pl
from jax.experimental.pallas import tpu as pltpu
from jax.sharding import PartitionSpec as P

EPS = 1e-05
HEADS = 6
C = 192
LOG2E = 1.4426950408889634
LN2 = 0.6931471805599453
SCALE = 32 ** (-0.5)
BF = jnp.bfloat16
F32 = jnp.float32
OWNERS = 16
HALF = 512
GROUPS = ((1, 0, 2), (3, 2, 1), (0, 3, 1))
MESH = pl.DeviceIdType.MESH


def nn(a, b):
    return lax.dot_general(a, b, (((1,), (0,)), ((), ())), preferred_element_type=F32)


def nt(a, b):
    return lax.dot_general(a, b, (((1,), (1,)), ((), ())), preferred_element_type=F32)


def tn(a, b):
    return lax.dot_general(a, b, (((0,), (0,)), ((), ())), preferred_element_type=F32)


def iota(shape, dim):
    return lax.broadcasted_iota(jnp.int32, shape, dim)


def one_hot(cond):
    return jnp.where(cond, 1.0, 0.0).astype(BF)


def lane_head():
    return ((iota((1, HALF), 1) & 63) * 57) >> 9


def lane_query():
    lane = iota((1, HALF), 1)
    return 9 * (lane >> 6) + (lane & 63) - 9 * lane_head()


def far_place(e):
    row = (e * 57) >> 10
    d = e - 56
    edge_row = (d * 43) >> 8
    return jnp.where(
        e < 54,
        24 * row + 6 + e - 18 * row,
        jnp.where((d >= 0) & (d < 18), 24 * edge_row + d - 6 * edge_row, -1),
    )


def join(one, two):
    tail = jnp.concatenate([one[:, 128:192], two[:, 128:192]], axis=1)
    return [v.astype(BF).reshape(10, 8, 128) for v in (one[:, 0:128], two[:, 0:128], tail)]


def split(ref, which):
    return jnp.concatenate(
        [ref[which].reshape(80, 128), ref[2].reshape(80, 128)[:, 64 * which : 64 * which + 64]], axis=1
    )


def make_kernel(lat_count, lon_count):
    def kernel(
        tok, cot, gain_hbm, win_hbm, wout_hbm, bias_ref, rb0, rb1, gr, near, edge,
        x, far, fs, fr, ps, gs, bias_v, bt0, bt1, perm, permb, choose, mask, pcs, pct,
        gain_ref, win_ref, wout_ref, wq, wk, wv, wqkt,
        standard, inverse, qbd, ubd, keys, vals, keyt, gq, gk, gv, ext, sb0, sb1,
        in_sem, own_sem, hs_sem, hr_sem, fs_sem, fr_sem, bs_sem, br_sem, gs_sem, gr_sem, keep_sem,
    ):
        lat = lax.axis_index("lat")
        lon = lax.axis_index("lon")
        half_count = lon_count // 2
        own_half = lon // half_count
        place = lax.rem(lon, half_count)
        other_half = 1 - own_half
        lat_next = lax.rem(lat + 1, lat_count)
        lat_prev = lax.rem(lat + lat_count - 1, lat_count)
        lon_next = lax.rem(lon + 1, lon_count)
        lon_prev = lax.rem(lon + lon_count - 1, lon_count)

        barrier = pltpu.get_barrier_semaphore()

        def greet(r, carry):
            pl.semaphore_signal(
                barrier, inc=1, device_id=(lat, lax.rem(lon + r, lon_count)), device_id_type=MESH
            )
            return carry

        for there in ((lat_prev, lon), (lat_next, lon), (lat_prev, lon_prev), (lat_next, lon_next)):
            pl.semaphore_signal(barrier, inc=1, device_id=there, device_id_type=MESH)
        lax.fori_loop(1, lon_count, greet, 0)

        own_copies, far_copies = [[], []], []
        for g, (src, z, count) in enumerate(GROUPS):
            for which, ref in enumerate((tok, cot)):
                copy = pltpu.make_async_copy(
                    ref.at[src : src + count, 0:3], far.at[which, z : z + count], own_sem.at[1, which, g]
                )
                copy.start()
                far_copies.append(copy)
        for g, (src, z, count) in enumerate(GROUPS):
            for which, ref in enumerate((tok, cot)):
                copy = pltpu.make_async_copy(
                    ref.at[src : src + count, 3:6],
                    x.at[which, z : z + count, :, 0:3],
                    own_sem.at[0, which, g],
                )
                copy.start()
                own_copies[min(g, 1)].append(copy)
        in_copies = [
            pltpu.make_async_copy(source, target, in_sem.at[i])
            for i, (source, target) in enumerate(
                (
                    (bias_ref.at[0], bias_v.at[0]),
                    (bias_ref.at[1], bias_v.at[1]),
                    (win_hbm, win_ref),
                    (wout_hbm, wout_ref),
                    (gain_hbm, gain_ref),
                )
            )
        ]
        for copy in in_copies:
            copy.start()

        ps[...] = one_hot(iota((80, 72), 1) == far_place(iota((80, 72), 0)))
        for copy in far_copies:
            copy.wait()
        for z in range(4):
            one, two = (nn(ps[...], far[which, z].reshape(72, C)) for which in range(2))
            for i, v in enumerate(join(one, two)):
                fs[z, i] = v

        pl.semaphore_wait(barrier, lon_count - 1 + 4)

        halo_copies = [[], []]
        for a in range(2):
            span = pl.ds(2 * a, 2)
            pieces = [
                (fs.at[span, :, 7:10], fr.at[span, :, 7:10], (lat_prev, lon_prev), fs_sem.at[a, 0], fr_sem.at[a, 0]),
                (fs.at[span, :, 0:7], fr.at[span, :, 0:7], (lat_prev, lon), fs_sem.at[a, 1], fr_sem.at[a, 1]),
            ]
            for g in ((1, 2) if a else (0,)):
                src, z, count = GROUPS[g]
                for which, ref in enumerate((tok, cot)):
                    pieces.append(
                        (
                            ref.at[src : src + count, 3:6, 0],
                            x.at[which, z : z + count, :, 3],
                            (lat, lon_prev),
                            hs_sem.at[which, g],
                            hr_sem.at[which, g],
                        )
                    )
            for source, target, there, send_sem, recv_sem in pieces:
                copy = pltpu.make_async_remote_copy(
                    src_ref=source,
                    dst_ref=target,
                    send_sem=send_sem,
                    recv_sem=recv_sem,
                    device_id=there,
                    device_id_type=MESH,
                )
                copy.start()
                halo_copies[a].append(copy)

        heads, queries = lane_head(), lane_query()
        perm[...] = one_hot(iota((128 * HEADS, HALF), 0) == 128 * heads + queries)
        permb[...] = one_hot(iota((72 * HEADS, HALF), 0) == 72 * heads + queries)
        choose[...] = one_hot((iota((72, HALF), 0) == queries) & (heads < HEADS))
        mask[...] = one_hot((iota((C, HALF), 0) >> 5) == heads)
        def grid_place(token):
            c = (token >= 72).astype(jnp.int32)
            inside = token - 72 * c
            row = (inside * 43) >> 9
            col = inside - 12 * row + 6 + 12 * c
            return jnp.where(
                row < 3,
                32 * row + col,
                96 + jnp.where(col < 24, 18 * row + col - 60, 6 * row + col + 14),
            )

        pcs[...] = one_hot(iota((144, 176), 1) == grid_place(iota((144, 176), 0)))
        pct[...] = one_hot(iota((176, 144), 0) == grid_place(iota((176, 144), 1)))
        for copy in in_copies:
            copy.wait()
        wq[...] = win_ref[:, 0:192]
        wk[...] = win_ref[:, 192:384]
        wv[...] = win_ref[:, 384:576]
        wqkt[0:192] = wq[...].astype(F32).T.astype(BF)
        wqkt[192:384] = wk[...].astype(F32).T.astype(BF)

        is_last = jnp.where(lat == lat_count - 1, -1e30, 0.0).astype(F32)
        query_late = queries >= 36

        def penalty(rows):
            return jnp.where((lax.rem(iota((rows, 1), 0), 72) >= 36) != query_late, is_last, 0.0)

        for a in range(2):
            for s in range(2):
                b = LOG2E * jnp.concatenate(
                    [bias_v[a, 144 * h + 72 * s : 144 * h + 72 * s + 72, :] for h in range(HEADS)], axis=0
                )
                high = b.astype(BF)
                low = (b - high.astype(F32)).astype(BF)
                moved = tn(high, permb[...]) + tn(low, permb[...])
                if a == 0:
                    bt0[s] = moved + penalty(144)
                else:
                    bt1[s] = moved[72 * s : 72 * s + 72] + penalty(72)

        gain = gain_ref[...]
        lane = iota((1, 128), 1) < 64
        blank = jnp.zeros((56, C), F32)

        def pad_pair(v):
            return jnp.concatenate([v[0:72], blank, v[72:144], blank], axis=0).astype(BF)

        def compact(sides):
            return jnp.concatenate(
                [
                    jnp.concatenate(
                        [side[32 * h : 32 * h + 32, 128 * c : 128 * c + 128] for h in range(HEADS)], axis=1
                    )
                    for side in sides
                    for c in range(2)
                ],
                axis=0,
            )

        def expand(target, wide):
            for l in range(2):
                for c in range(2):
                    at = 32 * (2 * l + c)
                    target[l, c] = jnp.concatenate([wide[at : at + 32]] * HEADS, axis=0) * mask[...]

        def prepare(a):
            ts, cts = (
                [
                    nn(
                        pcs[...],
                        jnp.concatenate(
                            [x[which, 2 * a + l].reshape(96, C), split(fr.at[2 * a + l], which)], axis=0
                        ),
                    )
                    for l in range(2)
                ]
                for which in range(2)
            )
            yield
            uts = [nt(wout_ref[...], pad_pair(cts[l])).astype(BF) for l in range(2)]
            plain = []
            for l in range(2):
                centred = ts[l] - jnp.sum(ts[l], axis=-1, keepdims=True) * (1.0 / C)
                inv = lax.rsqrt(jnp.sum(centred * centred, axis=-1, keepdims=True) * (1.0 / C) + EPS)
                unit = centred * inv
                inverse[a, l] = inv
                standard[a, l] = unit
                plain.append(unit * gain)
            yield
            expand(ubd.at[a], nn(compact(uts), perm[...]).astype(BF))
            yield
            qts = []
            for l in range(2):
                projected = nt(wqkt[...] if a else wqkt[0:192], pad_pair(plain[l]))
                qts.append((projected[0:192] * (SCALE * LOG2E)).astype(BF))
                if a:
                    for c in range(2):
                        keyt[2 + 2 * l + c, :, 0:72] = (
                            projected[192:384, 128 * c : 128 * c + 72] * SCALE
                        ).astype(BF)
            yield
            together = jnp.concatenate(plain, axis=0).astype(BF)
            for target, weight in ((keys, wk), (vals, wv)):
                rows = nn(together, weight[...])
                for c in range(2):
                    if a:
                        for l in range(2):
                            at = 144 * l + 72 * c
                            target[2 + 2 * l + c, 0:72] = rows[at : at + 72].astype(BF)
                    else:
                        target[c] = jnp.concatenate(
                            [rows[72 * c : 72 * c + 72], rows[144 + 72 * c : 216 + 72 * c]], axis=0
                        ).astype(BF)
            if not a:
                for c in range(2):
                    whole = jnp.concatenate([v[72 * c : 72 * c + 72] for v in plain], axis=0).astype(BF)
                    keyt[c] = (nt(wqkt[192:384], whole) * SCALE).astype(BF)
            yield
            expand(qbd.at[a], nn(compact(qts), perm[...]).astype(BF))
            yield

        sums = {}
        parts = {}

        def block(a, s, c):
            if a:
                at = 2 + 2 * s + c
                k, v, kt, biast = keys[at, 0:72], vals[at, 0:72], keyt[at, :, 0:72], bt1[s]
            else:
                k, v, kt, biast = keys[c], vals[c], keyt[c], bt0[s]
            scores = nn(k, qbd[a, s, c])
            dprobs = nn(v, ubd[a, s, c])
            yield
            e = jnp.exp2(scores + biast)
            probs = e * (1.0 / jnp.sum(e, axis=0, keepdims=True))
            weighted = probs * dprobs
            dscores = weighted - probs * jnp.sum(weighted, axis=0, keepdims=True)
            sums[a, s] = dscores if c == 0 else sums[a, s] + dscores
            low = dscores.astype(BF)
            dv = nt(probs.astype(BF), ubd[a, s, c])
            wide = nn(kt, low)
            dk = nt(low, qbd[a, s, c]) * LN2
            if a:
                gk[a, s, c] = dk
                gv[a, s, c] = dv
            elif s == 0:
                parts[c] = (dk, dv)
            else:
                for target, total in ((gk, parts[c][0] + dk), (gv, parts[c][1] + dv)):
                    for l in range(2):
                        target[a, l, c] = total[72 * l : 72 * l + 72]
            yield
            gq[a, s, c] = nt(choose[...], wide.astype(BF) * mask[...])
            yield

        def pack(a, s):
            for tile in range(4):
                part = sums[a, s][:, 128 * tile : 128 * tile + 128]
                target, top, bottom = (sb1, part[0:40], part[32:72]) if a else (sb0, part[0:72], part[72:144])
                owner = 8 * s + 2 * tile
                target[owner] = jnp.where(lane, top, pltpu.roll(bottom, 64, 1)).astype(BF)
                target[owner + 1] = jnp.where(lane, pltpu.roll(top, 64, 1), bottom).astype(BF)

        def finish(a):
            dq, dk, dv = (ref[a].reshape(288, C).astype(BF) for ref in (gq, gk, gv))
            scaled = (nt(dq, wq[...]) + nt(dk, wk[...]) + nt(dv, wv[...])) * gain
            yield
            away = []
            for l in range(2):
                part = scaled[144 * l : 144 * l + 144]
                unit = standard[a, l]
                grad = inverse[a, l] * (
                    part
                    - jnp.sum(part, axis=-1, keepdims=True) * (1.0 / C)
                    - unit * (jnp.sum(part * unit, axis=-1, keepdims=True) * (1.0 / C))
                )
                full = nn(pct[...], grad.astype(BF))
                ext[(2 * a + l + 1) % 4] = full[0:96].reshape(3, 4, 8, C).astype(BF)
                away.append(full[96:176])
            for i, v in enumerate(join(*away)):
                gs[a, i] = v
            yield

        def send_grads(a):
            pieces = [
                (gs.at[a, :, 0:7], gr.at[a, :, 0:7], (lat_next, lon), gs_sem.at[a, 0], gr_sem.at[a, 0]),
                (gs.at[a, :, 7:10], gr.at[a, :, 7:10], (lat_next, lon_next), gs_sem.at[a, 1], gr_sem.at[a, 1]),
            ]
            copies = []
            for g in ((1, 2) if a else (0,)):
                level, _, count = GROUPS[g]
                span = pl.ds(level, count)
                pieces.append(
                    (ext.at[span, :, 3], edge.at[span], (lat, lon_next), gs_sem.at[2, g], gr_sem.at[2, g])
                )
                copies.append(pltpu.make_async_copy(ext.at[span, :, 0:3], near.at[span], keep_sem.at[g]))
            copies = [
                pltpu.make_async_remote_copy(
                    src_ref=source,
                    dst_ref=target,
                    send_sem=send_sem,
                    recv_sem=recv_sem,
                    device_id=there,
                    device_id_type=MESH,
                )
                for source, target, there, send_sem, recv_sem in pieces
            ] + copies
            for copy in copies:
                copy.start()
            return copies

        def bias_copy(a, slot):
            half = other_half if slot >= half_count else own_half
            there = half_count * half + ((place + slot) & (half_count - 1))
            source, target = ((sb0, rb0), (sb1, rb1))[a]
            return pltpu.make_async_remote_copy(
                src_ref=source.at[there],
                dst_ref=target.at[slot],
                send_sem=bs_sem.at[a, slot],
                recv_sem=br_sem.at[a, slot],
                device_id=(lat, there),
                device_id_type=MESH,
            )

        def keep_copy(a):
            source, target = ((sb0, rb0), (sb1, rb1))[a]
            return pltpu.make_async_copy(source.at[lon], target.at[0], keep_sem.at[3 + a])

        def send_bias(a):
            for slot in range(half_count, lon_count):
                bias_copy(a, slot).start()
            for slot in range(1, half_count):
                bias_copy(a, slot).start()
            keep_copy(a).start()

        def arrived(g):
            for copy in own_copies[g] + halo_copies[g]:
                copy.wait()

        def run(*pieces):
            for piece in pieces:
                next(piece)

        p0, p1, f0, f1 = prepare(0), prepare(1), finish(0), finish(1)
        b0, b1, b2, b3 = (block(0, s, c) for s in range(2) for c in range(2))
        b4, b5, b6, b7 = (block(1, s, c) for s in range(2) for c in range(2))
        arrived(0)
        run(*[p0] * 6)
        arrived(1)
        run(p1, b0, b1, p1, p1, b0, b2, p1, b1, b0, b3, p1, b1)
        pack(0, 0)
        run(p1, b2, b4, b2, b3, b5, b3)
        pack(0, 1)
        send_bias(0)
        run(f0, b4, b6, f0)
        grad_copies = send_grads(0)
        run(b4, b5, b7, b5, b6, b6, b7, b7, f1, f1)
        grad_copies += send_grads(1)
        pack(1, 0)
        pack(1, 1)
        send_bias(1)

        for copy in grad_copies:
            copy.wait()
        for a in range(2):
            keep_copy(a).wait()

        for a in range(2):
            for slot in range(1, lon_count):
                bias_copy(a, slot).wait()

    return kernel


def make_final(lon_count):
    def final(rb0, rb1, gr, near, edge, out_ref, bout_ref):
        lane = iota((1, 128), 1) < 64
        out_ref[:, 3:6, 1:3] = near[:, :, 1:3]
        out_ref[:, 3:6, 0] = near[:, :, 0] + edge[...]
        back = one_hot(iota((72, 80), 0) == far_place(iota((72, 80), 1)))
        for a in range(2):
            for l in range(2):
                rows = nn(back, split(gr.at[a], l))
                out_ref[(2 * a + l + 1) % 4, 0:3] = rows.reshape(3, 3, 8, C).astype(BF)
        sum0, sum1 = rb0[0].astype(F32), rb1[0].astype(F32)
        for slot in range(1, lon_count):
            sum0 += rb0[slot].astype(F32)
            sum1 += rb1[slot].astype(F32)
        first = jnp.concatenate([sum0, pltpu.roll(sum0, 64, 1)], axis=0)
        second = jnp.concatenate([pltpu.roll(sum1, 64, 1), sum1[8:40]], axis=0)
        early = lax.axis_index("lon") < lon_count // 2
        second = jnp.concatenate(
            [jnp.where(early, second, 0.0), jnp.where(early, 0.0, second)], axis=0
        )
        both = jnp.where(lane, first, second).T
        for a in range(2):
            for h in range(HEADS):
                for q in range(9):
                    at = 64 * a + 9 * h + q
                    bout_ref[a, h, q] = both[at : at + 1]

    return final


def make_local(lat_count, lon_count):
    def local(tokens, cotangent, norm_gain, inproj_weight, outproj_weight, bias):
        any_spec = pl.BlockSpec(memory_space=pl.ANY)
        vmem = pl.BlockSpec(memory_space=pltpu.VMEM)
        dma = pltpu.SemaphoreType.DMA
        parts = pl.pallas_call(
            make_kernel(lat_count, lon_count),
            out_shape=(
                pltpu.VMEM((OWNERS, 72, 128), BF),
                pltpu.VMEM((OWNERS, 40, 128), BF),
                pltpu.VMEM((2, 3, 10, 8, 128), BF),
                pltpu.VMEM((4, 3, 3, 8, C), BF),
                pltpu.VMEM((4, 3, 8, C), BF),
            ),
            in_specs=[any_spec] * 6,
            out_specs=(any_spec,) * 5,
            scratch_shapes=[
                pltpu.VMEM((2, 4, 3, 4, 8, C), BF),
                pltpu.VMEM((2, 4, 3, 3, 8, C), BF),
                pltpu.VMEM((4, 3, 10, 8, 128), BF),
                pltpu.VMEM((4, 3, 10, 8, 128), BF),
                pltpu.VMEM((80, 72), BF),
                pltpu.VMEM((2, 3, 10, 8, 128), BF),
                pltpu.VMEM((2, 864, 144), F32),
                pltpu.VMEM((2, 144, HALF), F32),
                pltpu.VMEM((2, 72, HALF), F32),
                pltpu.VMEM((128 * HEADS, HALF), BF),
                pltpu.VMEM((72 * HEADS, HALF), BF),
                pltpu.VMEM((72, HALF), BF),
                pltpu.VMEM((C, HALF), BF),
                pltpu.VMEM((144, 176), BF),
                pltpu.VMEM((176, 144), BF),
                pltpu.VMEM((1, C), F32),
                pltpu.VMEM((C, 3 * C), BF),
                pltpu.VMEM((C, C), BF),
            ]
            + [pltpu.VMEM((C, C), BF)] * 3
            + [
                pltpu.VMEM((2 * C, C), BF),
                pltpu.VMEM((2, 2, 144, C), F32),
                pltpu.VMEM((2, 2, 144, 1), F32),
                pltpu.VMEM((2, 2, 2, C, HALF), BF),
                pltpu.VMEM((2, 2, 2, C, HALF), BF),
                pltpu.VMEM((6, 144, C), BF),
                pltpu.VMEM((6, 144, C), BF),
                pltpu.VMEM((6, C, 144), BF),
                pltpu.VMEM((2, 2, 2, 72, C), F32),
                pltpu.VMEM((2, 2, 2, 72, C), F32),
                pltpu.VMEM((2, 2, 2, 72, C), F32),
                pltpu.VMEM((4, 3, 4, 8, C), BF),
                pltpu.VMEM((OWNERS, 72, 128), BF),
                pltpu.VMEM((OWNERS, 40, 128), BF),
                dma((5,)),
                dma((2, 2, 3)),
                dma((2, 3)),
                dma((2, 3)),
                dma((2, 2)),
                dma((2, 2)),
                dma((2, OWNERS)),
                dma((2, OWNERS)),
                dma((3, 3)),
                dma((3, 3)),
                dma((5,)),
            ],
            compiler_params=pltpu.CompilerParams(collective_id=0, has_side_effects=True),
        )(
            tokens.reshape(4, 6, 3, 8, C),
            cotangent.reshape(4, 6, 3, 8, C),
            norm_gain.reshape(1, C),
            inproj_weight,
            outproj_weight,
            bias.reshape(2, 864, 144),
        )
        grad, bias_grad = pl.pallas_call(
            make_final(lon_count),
            out_shape=(
                jax.ShapeDtypeStruct((4, 6, 3, 8, C), BF),
                jax.ShapeDtypeStruct((2, HEADS, 9, 1, 144), F32),
            ),
            in_specs=[vmem] * 5,
            out_specs=(vmem, vmem),
            compiler_params=pltpu.CompilerParams(vmem_limit_bytes=8 * 1024 * 1024),
        )(*parts)
        return grad.reshape(4, 6, 24, C), bias_grad.reshape(2, 1, HEADS, 9, 144)

    return local


def solution(mesh):
    placed = (
        P(None, "lat", "lon", None),
        P(None, "lat", "lon", None),
        P(),
        P(),
        P(),
        P(None, "lat", None, None, None),
    )
    return jax.shard_map(
        make_local(mesh.shape["lat"], mesh.shape["lon"]),
        mesh=mesh,
        in_specs=placed,
        out_specs=(P(None, "lat", "lon", None), P(None, "lat", None, "lon", None)),
        check_vma=False,
    )
```

```python
import jax
import jax.numpy as jnp
from jax import lax
from jax.experimental import pallas as pl
from jax.experimental.pallas import tpu as pltpu
from jax.sharding import PartitionSpec as P

EPS = 1e-05
HEADS = 6
C = 192
LOG2E = 1.4426950408889634
LN2 = 0.6931471805599453
SCALE = 32 ** (-0.5)
BF = jnp.bfloat16
F32 = jnp.float32
OWNERS = 16
HALF = 512
GROUPS = ((1, 0, 2), (3, 2, 1), (0, 3, 1))
MESH = pl.DeviceIdType.MESH


def nn(a, b):
    return lax.dot_general(a, b, (((1,), (0,)), ((), ())), preferred_element_type=F32)


def nt(a, b):
    return lax.dot_general(a, b, (((1,), (1,)), ((), ())), preferred_element_type=F32)


def tn(a, b):
    return lax.dot_general(a, b, (((0,), (0,)), ((), ())), preferred_element_type=F32)


def iota(shape, dim):
    return lax.broadcasted_iota(jnp.int32, shape, dim)


def one_hot(cond):
    return jnp.where(cond, 1.0, 0.0).astype(BF)


def lane_head():
    return ((iota((1, HALF), 1) & 63) * 57) >> 9


def lane_query():
    lane = iota((1, HALF), 1)
    return 9 * (lane >> 6) + (lane & 63) - 9 * lane_head()


def far_place(e):
    row = (e * 57) >> 10
    d = e - 56
    edge_row = (d * 43) >> 8
    return jnp.where(
        e < 54,
        24 * row + 6 + e - 18 * row,
        jnp.where((d >= 0) & (d < 18), 24 * edge_row + d - 6 * edge_row, -1),
    )


def join(one, two):
    tail = jnp.concatenate([one[:, 128:192], two[:, 128:192]], axis=1)
    return [v.astype(BF).reshape(10, 8, 128) for v in (one[:, 0:128], two[:, 0:128], tail)]


def split(ref, which):
    return jnp.concatenate(
        [ref[which].reshape(80, 128), ref[2].reshape(80, 128)[:, 64 * which : 64 * which + 64]], axis=1
    )


def make_kernel(lat_count, lon_count):
    def kernel(
        tok, cot, gain_hbm, win_hbm, wout_hbm, bias_ref, rb0, rb1, gr, near, edge,
        x, far, fs, fr, ps, gs, bias_v, bt0, bt1, perm, permb, choose, mask, pcs, pct,
        gain_ref, win_ref, wout_ref, wq, wk, wv, wqkt,
        standard, inverse, qbd, ubd, keys, vals, keyt, gq, gk, gv, ext, sb0, sb1,
        in_sem, own_sem, hs_sem, hr_sem, fs_sem, fr_sem, bs_sem, br_sem, gs_sem, gr_sem, keep_sem,
    ):
        lat = lax.axis_index("lat")
        lon = lax.axis_index("lon")
        half_count = lon_count // 2
        own_half = lon // half_count
        place = lax.rem(lon, half_count)
        other_half = 1 - own_half
        lat_next = lax.rem(lat + 1, lat_count)
        lat_prev = lax.rem(lat + lat_count - 1, lat_count)
        lon_next = lax.rem(lon + 1, lon_count)
        lon_prev = lax.rem(lon + lon_count - 1, lon_count)

        barrier = pltpu.get_barrier_semaphore()

        def greet(r, carry):
            pl.semaphore_signal(
                barrier, inc=1, device_id=(lat, lax.rem(lon + r, lon_count)), device_id_type=MESH
            )
            return carry

        for there in ((lat_prev, lon), (lat_next, lon), (lat_prev, lon_prev), (lat_next, lon_next)):
            pl.semaphore_signal(barrier, inc=1, device_id=there, device_id_type=MESH)
        lax.fori_loop(1, lon_count, greet, 0)

        own_copies, far_copies = [[], []], []
        for g, (src, z, count) in enumerate(GROUPS):
            for which, ref in enumerate((tok, cot)):
                copy = pltpu.make_async_copy(
                    ref.at[src : src + count, 0:3], far.at[which, z : z + count], own_sem.at[1, which, g]
                )
                copy.start()
                far_copies.append(copy)
        for g, (src, z, count) in enumerate(GROUPS):
            for which, ref in enumerate((tok, cot)):
                copy = pltpu.make_async_copy(
                    ref.at[src : src + count, 3:6],
                    x.at[which, z : z + count, :, 0:3],
                    own_sem.at[0, which, g],
                )
                copy.start()
                own_copies[min(g, 1)].append(copy)
        in_copies = [
            pltpu.make_async_copy(source, target, in_sem.at[i])
            for i, (source, target) in enumerate(
                (
                    (bias_ref.at[0], bias_v.at[0]),
                    (bias_ref.at[1], bias_v.at[1]),
                    (win_hbm, win_ref),
                    (wout_hbm, wout_ref),
                    (gain_hbm, gain_ref),
                )
            )
        ]
        for copy in in_copies:
            copy.start()

        ps[...] = one_hot(iota((80, 72), 1) == far_place(iota((80, 72), 0)))
        for copy in far_copies:
            copy.wait()
        for z in range(4):
            one, two = (nn(ps[...], far[which, z].reshape(72, C)) for which in range(2))
            for i, v in enumerate(join(one, two)):
                fs[z, i] = v

        pl.semaphore_wait(barrier, lon_count - 1 + 4)

        halo_copies = [[], []]
        for a in range(2):
            span = pl.ds(2 * a, 2)
            pieces = [
                (fs.at[span, :, 7:10], fr.at[span, :, 7:10], (lat_prev, lon_prev), fs_sem.at[a, 0], fr_sem.at[a, 0]),
                (fs.at[span, :, 0:7], fr.at[span, :, 0:7], (lat_prev, lon), fs_sem.at[a, 1], fr_sem.at[a, 1]),
            ]
            for g in ((1, 2) if a else (0,)):
                src, z, count = GROUPS[g]
                for which, ref in enumerate((tok, cot)):
                    pieces.append(
                        (
                            ref.at[src : src + count, 3:6, 0],
                            x.at[which, z : z + count, :, 3],
                            (lat, lon_prev),
                            hs_sem.at[which, g],
                            hr_sem.at[which, g],
                        )
                    )
            for source, target, there, send_sem, recv_sem in pieces:
                copy = pltpu.make_async_remote_copy(
                    src_ref=source,
                    dst_ref=target,
                    send_sem=send_sem,
                    recv_sem=recv_sem,
                    device_id=there,
                    device_id_type=MESH,
                )
                copy.start()
                halo_copies[a].append(copy)

        heads, queries = lane_head(), lane_query()
        perm[...] = one_hot(iota((128 * HEADS, HALF), 0) == 128 * heads + queries)
        permb[...] = one_hot(iota((72 * HEADS, HALF), 0) == 72 * heads + queries)
        choose[...] = one_hot((iota((72, HALF), 0) == queries) & (heads < HEADS))
        mask[...] = one_hot((iota((C, HALF), 0) >> 5) == heads)
        def grid_place(token):
            c = (token >= 72).astype(jnp.int32)
            inside = token - 72 * c
            row = (inside * 43) >> 9
            col = inside - 12 * row + 6 + 12 * c
            return jnp.where(
                row < 3,
                32 * row + col,
                96 + jnp.where(col < 24, 18 * row + col - 60, 6 * row + col + 14),
            )

        pcs[...] = one_hot(iota((144, 176), 1) == grid_place(iota((144, 176), 0)))
        pct[...] = one_hot(iota((176, 144), 0) == grid_place(iota((176, 144), 1)))
        for copy in in_copies:
            copy.wait()
        wq[...] = win_ref[:, 0:192]
        wk[...] = win_ref[:, 192:384]
        wv[...] = win_ref[:, 384:576]
        wqkt[0:192] = wq[...].astype(F32).T.astype(BF)
        wqkt[192:384] = wk[...].astype(F32).T.astype(BF)

        is_last = jnp.where(lat == lat_count - 1, -1e30, 0.0).astype(F32)
        query_late = queries >= 36

        def penalty(rows):
            return jnp.where((lax.rem(iota((rows, 1), 0), 72) >= 36) != query_late, is_last, 0.0)

        for a in range(2):
            for s in range(2):
                b = LOG2E * jnp.concatenate(
                    [bias_v[a, 144 * h + 72 * s : 144 * h + 72 * s + 72, :] for h in range(HEADS)], axis=0
                )
                high = b.astype(BF)
                low = (b - high.astype(F32)).astype(BF)
                moved = tn(high, permb[...]) + tn(low, permb[...])
                if a == 0:
                    bt0[s] = moved + penalty(144)
                else:
                    bt1[s] = moved[72 * s : 72 * s + 72] + penalty(72)

        gain = gain_ref[...]
        lane = iota((1, 128), 1) < 64
        blank = jnp.zeros((56, C), F32)

        def pad_pair(v):
            return jnp.concatenate([v[0:72], blank, v[72:144], blank], axis=0).astype(BF)

        def compact(sides):
            return jnp.concatenate(
                [
                    jnp.concatenate(
                        [side[32 * h : 32 * h + 32, 128 * c : 128 * c + 128] for h in range(HEADS)], axis=1
                    )
                    for side in sides
                    for c in range(2)
                ],
                axis=0,
            )

        def expand(target, wide):
            for l in range(2):
                for c in range(2):
                    at = 32 * (2 * l + c)
                    target[l, c] = jnp.concatenate([wide[at : at + 32]] * HEADS, axis=0) * mask[...]

        def prepare(a):
            ts, cts = (
                [
                    nn(
                        pcs[...],
                        jnp.concatenate(
                            [x[which, 2 * a + l].reshape(96, C), split(fr.at[2 * a + l], which)], axis=0
                        ),
                    )
                    for l in range(2)
                ]
                for which in range(2)
            )
            yield
            uts = [nt(wout_ref[...], pad_pair(cts[l])).astype(BF) for l in range(2)]
            plain = []
            for l in range(2):
                centred = ts[l] - jnp.sum(ts[l], axis=-1, keepdims=True) * (1.0 / C)
                inv = lax.rsqrt(jnp.sum(centred * centred, axis=-1, keepdims=True) * (1.0 / C) + EPS)
                unit = centred * inv
                inverse[a, l] = inv
                standard[a, l] = unit
                plain.append(unit * gain)
            yield
            expand(ubd.at[a], nn(compact(uts), perm[...]).astype(BF))
            yield
            qts = []
            for l in range(2):
                projected = nt(wqkt[...] if a else wqkt[0:192], pad_pair(plain[l]))
                qts.append((projected[0:192] * (SCALE * LOG2E)).astype(BF))
                if a:
                    for c in range(2):
                        keyt[2 + 2 * l + c, :, 0:72] = (
                            projected[192:384, 128 * c : 128 * c + 72] * SCALE
                        ).astype(BF)
            yield
            together = jnp.concatenate(plain, axis=0).astype(BF)
            for target, weight in ((keys, wk), (vals, wv)):
                rows = nn(together, weight[...])
                for c in range(2):
                    if a:
                        for l in range(2):
                            at = 144 * l + 72 * c
                            target[2 + 2 * l + c, 0:72] = rows[at : at + 72].astype(BF)
                    else:
                        target[c] = jnp.concatenate(
                            [rows[72 * c : 72 * c + 72], rows[144 + 72 * c : 216 + 72 * c]], axis=0
                        ).astype(BF)
            if not a:
                for c in range(2):
                    whole = jnp.concatenate([v[72 * c : 72 * c + 72] for v in plain], axis=0).astype(BF)
                    keyt[c] = (nt(wqkt[192:384], whole) * SCALE).astype(BF)
            yield
            expand(qbd.at[a], nn(compact(qts), perm[...]).astype(BF))
            yield

        sums = {}
        parts = {}

        halves = (other_half, own_half)

        def block(a, i, c):
            s = halves[i]
            if a:
                at = 2 + 2 * s + c
                k, v, kt, biast = keys[at, 0:72], vals[at, 0:72], keyt[at, :, 0:72], bt1[s]
            else:
                k, v, kt, biast = keys[c], vals[c], keyt[c], bt0[s]
            scores = nn(k, qbd[a, s, c])
            dprobs = nn(v, ubd[a, s, c])
            yield
            e = jnp.exp2(scores + biast)
            probs = e * (1.0 / jnp.sum(e, axis=0, keepdims=True))
            weighted = probs * dprobs
            dscores = weighted - probs * jnp.sum(weighted, axis=0, keepdims=True)
            sums[a, i] = dscores if c == 0 else sums[a, i] + dscores
            low = dscores.astype(BF)
            dv = nt(probs.astype(BF), ubd[a, s, c])
            wide = nn(kt, low)
            dk = nt(low, qbd[a, s, c]) * LN2
            if a:
                gk[a, s, c] = dk
                gv[a, s, c] = dv
            elif i == 0:
                parts[c] = (dk, dv)
            else:
                for target, total in ((gk, parts[c][0] + dk), (gv, parts[c][1] + dv)):
                    for l in range(2):
                        target[a, l, c] = total[72 * l : 72 * l + 72]
            yield
            gq[a, s, c] = nt(choose[...], wide.astype(BF) * mask[...])
            yield

        def pack(a, i):
            for tile in range(4):
                part = sums[a, i][:, 128 * tile : 128 * tile + 128]
                target, top, bottom = (sb1, part[0:40], part[32:72]) if a else (sb0, part[0:72], part[72:144])
                owner = 8 * halves[i] + 2 * tile
                target[owner] = jnp.where(lane, top, pltpu.roll(bottom, 64, 1)).astype(BF)
                target[owner + 1] = jnp.where(lane, pltpu.roll(top, 64, 1), bottom).astype(BF)

        def finish(a):
            dq, dk, dv = (ref[a].reshape(288, C).astype(BF) for ref in (gq, gk, gv))
            scaled = (nt(dq, wq[...]) + nt(dk, wk[...]) + nt(dv, wv[...])) * gain
            yield
            away = []
            for l in range(2):
                part = scaled[144 * l : 144 * l + 144]
                unit = standard[a, l]
                grad = inverse[a, l] * (
                    part
                    - jnp.sum(part, axis=-1, keepdims=True) * (1.0 / C)
                    - unit * (jnp.sum(part * unit, axis=-1, keepdims=True) * (1.0 / C))
                )
                full = nn(pct[...], grad.astype(BF))
                ext[(2 * a + l + 1) % 4] = full[0:96].reshape(3, 4, 8, C).astype(BF)
                away.append(full[96:176])
            for i, v in enumerate(join(*away)):
                gs[a, i] = v
            yield

        def send_grads(a):
            pieces = [
                (gs.at[a, :, 0:7], gr.at[a, :, 0:7], (lat_next, lon), gs_sem.at[a, 0], gr_sem.at[a, 0]),
                (gs.at[a, :, 7:10], gr.at[a, :, 7:10], (lat_next, lon_next), gs_sem.at[a, 1], gr_sem.at[a, 1]),
            ]
            copies = []
            for g in ((1, 2) if a else (0,)):
                level, _, count = GROUPS[g]
                span = pl.ds(level, count)
                pieces.append(
                    (ext.at[span, :, 3], edge.at[span], (lat, lon_next), gs_sem.at[2, g], gr_sem.at[2, g])
                )
                copies.append(pltpu.make_async_copy(ext.at[span, :, 0:3], near.at[span], keep_sem.at[g]))
            copies = [
                pltpu.make_async_remote_copy(
                    src_ref=source,
                    dst_ref=target,
                    send_sem=send_sem,
                    recv_sem=recv_sem,
                    device_id=there,
                    device_id_type=MESH,
                )
                for source, target, there, send_sem, recv_sem in pieces
            ] + copies
            for copy in copies:
                copy.start()
            return copies

        def bias_copy(a, slot):
            half = other_half if slot >= half_count else own_half
            there = half_count * half + ((place + slot) & (half_count - 1))
            source, target = ((sb0, rb0), (sb1, rb1))[a]
            return pltpu.make_async_remote_copy(
                src_ref=source.at[there],
                dst_ref=target.at[slot],
                send_sem=bs_sem.at[a, slot],
                recv_sem=br_sem.at[a, slot],
                device_id=(lat, there),
                device_id_type=MESH,
            )

        def keep_copy(a):
            source, target = ((sb0, rb0), (sb1, rb1))[a]
            return pltpu.make_async_copy(source.at[lon], target.at[0], keep_sem.at[3 + a])

        def send_bias(a, i):
            for slot in range(1, half_count) if i else range(half_count, lon_count):
                bias_copy(a, slot).start()
            if i:
                keep_copy(a).start()

        def arrived(g):
            for copy in own_copies[g] + halo_copies[g]:
                copy.wait()

        def run(*pieces):
            for piece in pieces:
                next(piece)

        p0, p1, f0, f1 = prepare(0), prepare(1), finish(0), finish(1)
        b0, b1, b2, b3 = (block(0, i, c) for i in range(2) for c in range(2))
        b4, b5, b6, b7 = (block(1, i, c) for i in range(2) for c in range(2))
        arrived(0)
        run(*[p0] * 6)
        arrived(1)
        run(p1, b0, b1, p1, p1, b0, b2, p1, b1, b0, b3, p1, b1)
        pack(0, 0)
        send_bias(0, 0)
        run(p1, b2, b4, b2, b3, b5, b3)
        pack(0, 1)
        send_bias(0, 1)
        run(f0, b4, b6, f0)
        grad_copies = send_grads(0)
        run(b4, b5, b7, b5, b6, b6, b7, b7, f1, f1)
        grad_copies += send_grads(1)
        pack(1, 0)
        pack(1, 1)
        send_bias(1, 0)
        send_bias(1, 1)

        for copy in grad_copies:
            copy.wait()
        for a in range(2):
            keep_copy(a).wait()

        for a in range(2):
            for slot in range(1, lon_count):
                bias_copy(a, slot).wait()

    return kernel


def make_final(lon_count):
    def final(rb0, rb1, gr, near, edge, out_ref, bout_ref):
        lane = iota((1, 128), 1) < 64
        out_ref[:, 3:6, 1:3] = near[:, :, 1:3]
        out_ref[:, 3:6, 0] = near[:, :, 0] + edge[...]
        back = one_hot(iota((72, 80), 0) == far_place(iota((72, 80), 1)))
        for a in range(2):
            for l in range(2):
                rows = nn(back, split(gr.at[a], l))
                out_ref[(2 * a + l + 1) % 4, 0:3] = rows.reshape(3, 3, 8, C).astype(BF)
        sum0, sum1 = rb0[0].astype(F32), rb1[0].astype(F32)
        for slot in range(1, lon_count):
            sum0 += rb0[slot].astype(F32)
            sum1 += rb1[slot].astype(F32)
        first = jnp.concatenate([sum0, pltpu.roll(sum0, 64, 1)], axis=0)
        second = jnp.concatenate([pltpu.roll(sum1, 64, 1), sum1[8:40]], axis=0)
        early = lax.axis_index("lon") < lon_count // 2
        second = jnp.concatenate(
            [jnp.where(early, second, 0.0), jnp.where(early, 0.0, second)], axis=0
        )
        both = jnp.where(lane, first, second).T
        for a in range(2):
            for h in range(HEADS):
                for q in range(9):
                    at = 64 * a + 9 * h + q
                    bout_ref[a, h, q] = both[at : at + 1]

    return final


def make_local(lat_count, lon_count):
    def local(tokens, cotangent, norm_gain, inproj_weight, outproj_weight, bias):
        any_spec = pl.BlockSpec(memory_space=pl.ANY)
        vmem = pl.BlockSpec(memory_space=pltpu.VMEM)
        dma = pltpu.SemaphoreType.DMA
        parts = pl.pallas_call(
            make_kernel(lat_count, lon_count),
            out_shape=(
                pltpu.VMEM((OWNERS, 72, 128), BF),
                pltpu.VMEM((OWNERS, 40, 128), BF),
                pltpu.VMEM((2, 3, 10, 8, 128), BF),
                pltpu.VMEM((4, 3, 3, 8, C), BF),
                pltpu.VMEM((4, 3, 8, C), BF),
            ),
            in_specs=[any_spec] * 6,
            out_specs=(any_spec,) * 5,
            scratch_shapes=[
                pltpu.VMEM((2, 4, 3, 4, 8, C), BF),
                pltpu.VMEM((2, 4, 3, 3, 8, C), BF),
                pltpu.VMEM((4, 3, 10, 8, 128), BF),
                pltpu.VMEM((4, 3, 10, 8, 128), BF),
                pltpu.VMEM((80, 72), BF),
                pltpu.VMEM((2, 3, 10, 8, 128), BF),
                pltpu.VMEM((2, 864, 144), F32),
                pltpu.VMEM((2, 144, HALF), F32),
                pltpu.VMEM((2, 72, HALF), F32),
                pltpu.VMEM((128 * HEADS, HALF), BF),
                pltpu.VMEM((72 * HEADS, HALF), BF),
                pltpu.VMEM((72, HALF), BF),
                pltpu.VMEM((C, HALF), BF),
                pltpu.VMEM((144, 176), BF),
                pltpu.VMEM((176, 144), BF),
                pltpu.VMEM((1, C), F32),
                pltpu.VMEM((C, 3 * C), BF),
                pltpu.VMEM((C, C), BF),
            ]
            + [pltpu.VMEM((C, C), BF)] * 3
            + [
                pltpu.VMEM((2 * C, C), BF),
                pltpu.VMEM((2, 2, 144, C), F32),
                pltpu.VMEM((2, 2, 144, 1), F32),
                pltpu.VMEM((2, 2, 2, C, HALF), BF),
                pltpu.VMEM((2, 2, 2, C, HALF), BF),
                pltpu.VMEM((6, 144, C), BF),
                pltpu.VMEM((6, 144, C), BF),
                pltpu.VMEM((6, C, 144), BF),
                pltpu.VMEM((2, 2, 2, 72, C), F32),
                pltpu.VMEM((2, 2, 2, 72, C), F32),
                pltpu.VMEM((2, 2, 2, 72, C), F32),
                pltpu.VMEM((4, 3, 4, 8, C), BF),
                pltpu.VMEM((OWNERS, 72, 128), BF),
                pltpu.VMEM((OWNERS, 40, 128), BF),
                dma((5,)),
                dma((2, 2, 3)),
                dma((2, 3)),
                dma((2, 3)),
                dma((2, 2)),
                dma((2, 2)),
                dma((2, OWNERS)),
                dma((2, OWNERS)),
                dma((3, 3)),
                dma((3, 3)),
                dma((5,)),
            ],
            compiler_params=pltpu.CompilerParams(collective_id=0, has_side_effects=True),
        )(
            tokens.reshape(4, 6, 3, 8, C),
            cotangent.reshape(4, 6, 3, 8, C),
            norm_gain.reshape(1, C),
            inproj_weight,
            outproj_weight,
            bias.reshape(2, 864, 144),
        )
        grad, bias_grad = pl.pallas_call(
            make_final(lon_count),
            out_shape=(
                jax.ShapeDtypeStruct((4, 6, 3, 8, C), BF),
                jax.ShapeDtypeStruct((2, HEADS, 9, 1, 144), F32),
            ),
            in_specs=[vmem] * 5,
            out_specs=(vmem, vmem),
            compiler_params=pltpu.CompilerParams(vmem_limit_bytes=8 * 1024 * 1024),
        )(*parts)
        return grad.reshape(4, 6, 24, C), bias_grad.reshape(2, 1, HEADS, 9, 144)

    return local


def solution(mesh):
    placed = (
        P(None, "lat", "lon", None),
        P(None, "lat", "lon", None),
        P(),
        P(),
        P(),
        P(None, "lat", None, None, None),
    )
    return jax.shard_map(
        make_local(mesh.shape["lat"], mesh.shape["lon"]),
        mesh=mesh,
        in_specs=placed,
        out_specs=(P(None, "lat", "lon", None), P(None, "lat", None, "lon", None)),
        check_vma=False,
    )
```

```python
import jax
import jax.numpy as jnp
from jax import lax
from jax.experimental import pallas as pl
from jax.experimental.pallas import tpu as pltpu
from jax.sharding import PartitionSpec as P

EPS = 1e-05
HEADS = 6
C = 192
LOG2E = 1.4426950408889634
LN2 = 0.6931471805599453
SCALE = 32 ** (-0.5)
BF = jnp.bfloat16
F32 = jnp.float32
OWNERS = 16
HALF = 512
GROUPS = ((1, 0, 2), (3, 2, 1), (0, 3, 1))
MESH = pl.DeviceIdType.MESH


def nn(a, b):
    return lax.dot_general(a, b, (((1,), (0,)), ((), ())), preferred_element_type=F32)


def nt(a, b):
    return lax.dot_general(a, b, (((1,), (1,)), ((), ())), preferred_element_type=F32)


def tn(a, b):
    return lax.dot_general(a, b, (((0,), (0,)), ((), ())), preferred_element_type=F32)


def iota(shape, dim):
    return lax.broadcasted_iota(jnp.int32, shape, dim)


def one_hot(cond):
    return jnp.where(cond, 1.0, 0.0).astype(BF)


def lane_head():
    return ((iota((1, HALF), 1) & 63) * 57) >> 9


def lane_query():
    lane = iota((1, HALF), 1)
    return 9 * (lane >> 6) + (lane & 63) - 9 * lane_head()


def far_place(e):
    row = (e * 57) >> 10
    d = e - 56
    edge_row = (d * 43) >> 8
    return jnp.where(
        e < 54,
        24 * row + 6 + e - 18 * row,
        jnp.where((d >= 0) & (d < 18), 24 * edge_row + d - 6 * edge_row, -1),
    )


def join(one, two):
    tail = jnp.concatenate([one[:, 128:192], two[:, 128:192]], axis=1)
    return [v.astype(BF).reshape(10, 8, 128) for v in (one[:, 0:128], two[:, 0:128], tail)]


def split(ref, which):
    return jnp.concatenate(
        [ref[which].reshape(80, 128), ref[2].reshape(80, 128)[:, 64 * which : 64 * which + 64]], axis=1
    )


def make_kernel(lat_count, lon_count):
    def kernel(
        tok, cot, gain_hbm, win_hbm, wout_hbm, bias_ref, rb0, rb1, gr, near, edge,
        x, far, fs, fr, ps, gs, bias_v, bt0, bt1, perm, permb, choose, mask, pcs, pct,
        gain_ref, win_ref, wout_ref, wq, wk, wv, wqkt,
        standard, inverse, qbd, ubd, keys, vals, keyt, gq, gk, gv, ext, sb0, sb1,
        in_sem, own_sem, hs_sem, hr_sem, fs_sem, fr_sem, bs_sem, br_sem, gs_sem, gr_sem, keep_sem,
    ):
        lat = lax.axis_index("lat")
        lon = lax.axis_index("lon")
        half_count = lon_count // 2
        own_half = lon // half_count
        place = lax.rem(lon, half_count)
        other_half = 1 - own_half
        lat_next = lax.rem(lat + 1, lat_count)
        lat_prev = lax.rem(lat + lat_count - 1, lat_count)
        lon_next = lax.rem(lon + 1, lon_count)
        lon_prev = lax.rem(lon + lon_count - 1, lon_count)

        barrier = pltpu.get_barrier_semaphore()

        def greet(r, carry):
            pl.semaphore_signal(
                barrier, inc=1, device_id=(lat, lax.rem(lon + r, lon_count)), device_id_type=MESH
            )
            return carry

        for there in ((lat_prev, lon), (lat_next, lon), (lat_prev, lon_prev), (lat_next, lon_next)):
            pl.semaphore_signal(barrier, inc=1, device_id=there, device_id_type=MESH)
        lax.fori_loop(1, lon_count, greet, 0)

        own_copies, far_copies = [[], []], []
        for g, (src, z, count) in enumerate(GROUPS):
            for which, ref in enumerate((tok, cot)):
                copy = pltpu.make_async_copy(
                    ref.at[src : src + count, 0:3], far.at[which, z : z + count], own_sem.at[1, which, g]
                )
                copy.start()
                far_copies.append(copy)
        for g, (src, z, count) in enumerate(GROUPS):
            for which, ref in enumerate((tok, cot)):
                copy = pltpu.make_async_copy(
                    ref.at[src : src + count, 3:6],
                    x.at[which, z : z + count, :, 0:3],
                    own_sem.at[0, which, g],
                )
                copy.start()
                own_copies[min(g, 1)].append(copy)
        in_copies = [
            pltpu.make_async_copy(source, target, in_sem.at[i])
            for i, (source, target) in enumerate(
                (
                    (bias_ref.at[0], bias_v.at[0]),
                    (bias_ref.at[1], bias_v.at[1]),
                    (win_hbm, win_ref),
                    (wout_hbm, wout_ref),
                    (gain_hbm, gain_ref),
                )
            )
        ]
        for copy in in_copies:
            copy.start()

        ps[...] = one_hot(iota((80, 72), 1) == far_place(iota((80, 72), 0)))
        for copy in far_copies:
            copy.wait()
        for z in range(4):
            one, two = (nn(ps[...], far[which, z].reshape(72, C)) for which in range(2))
            for i, v in enumerate(join(one, two)):
                fs[z, i] = v

        pl.semaphore_wait(barrier, lon_count - 1 + 4)

        halo_copies = [[], []]
        for a in range(2):
            span = pl.ds(2 * a, 2)
            pieces = [
                (fs.at[span, :, 7:10], fr.at[span, :, 7:10], (lat_prev, lon_prev), fs_sem.at[a, 0], fr_sem.at[a, 0]),
                (fs.at[span, :, 0:7], fr.at[span, :, 0:7], (lat_prev, lon), fs_sem.at[a, 1], fr_sem.at[a, 1]),
            ]
            for g in ((1, 2) if a else (0,)):
                src, z, count = GROUPS[g]
                for which, ref in enumerate((tok, cot)):
                    pieces.append(
                        (
                            ref.at[src : src + count, 3:6, 0],
                            x.at[which, z : z + count, :, 3],
                            (lat, lon_prev),
                            hs_sem.at[which, g],
                            hr_sem.at[which, g],
                        )
                    )
            for source, target, there, send_sem, recv_sem in pieces:
                copy = pltpu.make_async_remote_copy(
                    src_ref=source,
                    dst_ref=target,
                    send_sem=send_sem,
                    recv_sem=recv_sem,
                    device_id=there,
                    device_id_type=MESH,
                )
                copy.start()
                halo_copies[a].append(copy)

        heads, queries = lane_head(), lane_query()
        perm[...] = one_hot(iota((128 * HEADS, HALF), 0) == 128 * heads + queries)
        permb[...] = one_hot(iota((72 * HEADS, HALF), 0) == 72 * heads + queries)
        choose[...] = one_hot((iota((72, HALF), 0) == queries) & (heads < HEADS))
        mask[...] = one_hot((iota((C, HALF), 0) >> 5) == heads)
        def grid_place(token):
            c = (token >= 72).astype(jnp.int32)
            inside = token - 72 * c
            row = (inside * 43) >> 9
            col = inside - 12 * row + 6 + 12 * c
            return jnp.where(
                row < 3,
                32 * row + col,
                96 + jnp.where(col < 24, 18 * row + col - 60, 6 * row + col + 14),
            )

        pcs[...] = one_hot(iota((144, 176), 1) == grid_place(iota((144, 176), 0)))
        pct[...] = one_hot(iota((176, 144), 0) == grid_place(iota((176, 144), 1)))
        for copy in in_copies:
            copy.wait()
        wq[...] = win_ref[:, 0:192]
        wk[...] = win_ref[:, 192:384]
        wv[...] = win_ref[:, 384:576]
        wqkt[0:192] = wq[...].astype(F32).T.astype(BF)
        wqkt[192:384] = wk[...].astype(F32).T.astype(BF)

        is_last = jnp.where(lat == lat_count - 1, -1e30, 0.0).astype(F32)
        query_late = queries >= 36

        def penalty(rows):
            return jnp.where((lax.rem(iota((rows, 1), 0), 72) >= 36) != query_late, is_last, 0.0)

        for a in range(2):
            for s in range(2):
                b = LOG2E * jnp.concatenate(
                    [bias_v[a, 144 * h + 72 * s : 144 * h + 72 * s + 72, :] for h in range(HEADS)], axis=0
                )
                high = b.astype(BF)
                low = (b - high.astype(F32)).astype(BF)
                moved = tn(high, permb[...]) + tn(low, permb[...])
                if a == 0:
                    bt0[s] = moved + penalty(144)
                else:
                    bt1[s] = moved[72 * s : 72 * s + 72] + penalty(72)

        gain = gain_ref[...]
        lane = iota((1, 128), 1) < 64
        blank = jnp.zeros((56, C), F32)

        def pad_pair(v):
            return jnp.concatenate([v[0:72], blank, v[72:144], blank], axis=0).astype(BF)

        def compact(sides):
            return jnp.concatenate(
                [
                    jnp.concatenate(
                        [side[32 * h : 32 * h + 32, 128 * c : 128 * c + 128] for h in range(HEADS)], axis=1
                    )
                    for side in sides
                    for c in range(2)
                ],
                axis=0,
            )

        def expand(target, wide):
            for l in range(2):
                for c in range(2):
                    at = 32 * (2 * l + c)
                    target[l, c] = jnp.concatenate([wide[at : at + 32]] * HEADS, axis=0) * mask[...]

        def prepare(a):
            ts, cts = (
                [
                    nn(
                        pcs[...],
                        jnp.concatenate(
                            [x[which, 2 * a + l].reshape(96, C), split(fr.at[2 * a + l], which)], axis=0
                        ),
                    )
                    for l in range(2)
                ]
                for which in range(2)
            )
            yield
            uts = [nt(wout_ref[...], pad_pair(cts[l])).astype(BF) for l in range(2)]
            plain = []
            for l in range(2):
                centred = ts[l] - jnp.sum(ts[l], axis=-1, keepdims=True) * (1.0 / C)
                inv = lax.rsqrt(jnp.sum(centred * centred, axis=-1, keepdims=True) * (1.0 / C) + EPS)
                unit = centred * inv
                inverse[a, l] = inv
                standard[a, l] = unit
                plain.append(unit * gain)
            yield
            expand(ubd.at[a], nn(compact(uts), perm[...]).astype(BF))
            yield
            qts = []
            for l in range(2):
                projected = nt(wqkt[...] if a else wqkt[0:192], pad_pair(plain[l]))
                qts.append((projected[0:192] * (SCALE * LOG2E)).astype(BF))
                if a:
                    for c in range(2):
                        keyt[2 + 2 * l + c, :, 0:72] = (
                            projected[192:384, 128 * c : 128 * c + 72] * SCALE
                        ).astype(BF)
            yield
            together = jnp.concatenate(plain, axis=0).astype(BF)
            for target, weight in ((keys, wk), (vals, wv)):
                rows = nn(together, weight[...])
                for c in range(2):
                    if a:
                        for l in range(2):
                            at = 144 * l + 72 * c
                            target[2 + 2 * l + c, 0:72] = rows[at : at + 72].astype(BF)
                    else:
                        target[c] = jnp.concatenate(
                            [rows[72 * c : 72 * c + 72], rows[144 + 72 * c : 216 + 72 * c]], axis=0
                        ).astype(BF)
            if not a:
                for c in range(2):
                    whole = jnp.concatenate([v[72 * c : 72 * c + 72] for v in plain], axis=0).astype(BF)
                    keyt[c] = (nt(wqkt[192:384], whole) * SCALE).astype(BF)
            yield
            expand(qbd.at[a], nn(compact(qts), perm[...]).astype(BF))
            yield

        sums = {}
        parts = {}

        halves = (other_half, own_half)

        def block(a, i, c):
            s = halves[i]
            if a:
                at = 2 + 2 * s + c
                k, v, kt, biast = keys[at, 0:72], vals[at, 0:72], keyt[at, :, 0:72], bt1[s]
            else:
                k, v, kt, biast = keys[c], vals[c], keyt[c], bt0[s]
            scores = nn(k, qbd[a, s, c])
            dprobs = nn(v, ubd[a, s, c])
            yield
            e = jnp.exp2(scores + biast)
            probs = e * (1.0 / jnp.sum(e, axis=0, keepdims=True))
            weighted = probs * dprobs
            dscores = weighted - probs * jnp.sum(weighted, axis=0, keepdims=True)
            sums[a, i] = dscores if c == 0 else sums[a, i] + dscores
            low = dscores.astype(BF)
            dv = nt(probs.astype(BF), ubd[a, s, c])
            wide = nn(kt, low)
            dk = nt(low, qbd[a, s, c]) * LN2
            if a:
                gk[a, s, c] = dk
                gv[a, s, c] = dv
            elif i == 0:
                parts[c] = (dk, dv)
            else:
                for target, total in ((gk, parts[c][0] + dk), (gv, parts[c][1] + dv)):
                    for l in range(2):
                        target[a, l, c] = total[72 * l : 72 * l + 72]
            yield
            gq[a, s, c] = nt(choose[...], wide.astype(BF) * mask[...])
            yield

        def pack(a, i):
            for tile in range(4):
                part = sums[a, i][:, 128 * tile : 128 * tile + 128]
                target, top, bottom = (sb1, part[0:40], part[32:72]) if a else (sb0, part[0:72], part[72:144])
                owner = 8 * halves[i] + 2 * tile
                target[owner] = jnp.where(lane, top, pltpu.roll(bottom, 64, 1)).astype(BF)
                target[owner + 1] = jnp.where(lane, pltpu.roll(top, 64, 1), bottom).astype(BF)

        def finish(a):
            dq, dk, dv = (ref[a].reshape(288, C).astype(BF) for ref in (gq, gk, gv))
            scaled = (nt(dq, wq[...]) + nt(dk, wk[...]) + nt(dv, wv[...])) * gain
            yield
            away = []
            for l in range(2):
                part = scaled[144 * l : 144 * l + 144]
                unit = standard[a, l]
                grad = inverse[a, l] * (
                    part
                    - jnp.sum(part, axis=-1, keepdims=True) * (1.0 / C)
                    - unit * (jnp.sum(part * unit, axis=-1, keepdims=True) * (1.0 / C))
                )
                full = nn(pct[...], grad.astype(BF))
                ext[(2 * a + l + 1) % 4] = full[0:96].reshape(3, 4, 8, C).astype(BF)
                away.append(full[96:176])
            for i, v in enumerate(join(*away)):
                gs[a, i] = v
            yield

        def send_grads(a):
            pieces = [
                (gs.at[a, :, 0:7], gr.at[a, :, 0:7], (lat_next, lon), gs_sem.at[a, 0], gr_sem.at[a, 0]),
                (gs.at[a, :, 7:10], gr.at[a, :, 7:10], (lat_next, lon_next), gs_sem.at[a, 1], gr_sem.at[a, 1]),
            ]
            copies = []
            for g in ((1, 2) if a else (0,)):
                level, _, count = GROUPS[g]
                span = pl.ds(level, count)
                pieces.append(
                    (ext.at[span, :, 3], edge.at[span], (lat, lon_next), gs_sem.at[2, g], gr_sem.at[2, g])
                )
                copies.append(pltpu.make_async_copy(ext.at[span, :, 0:3], near.at[span], keep_sem.at[g]))
            copies = [
                pltpu.make_async_remote_copy(
                    src_ref=source,
                    dst_ref=target,
                    send_sem=send_sem,
                    recv_sem=recv_sem,
                    device_id=there,
                    device_id_type=MESH,
                )
                for source, target, there, send_sem, recv_sem in pieces
            ] + copies
            for copy in copies:
                copy.start()
            return copies

        def bias_copy(a, slot):
            half = other_half if slot >= half_count else own_half
            there = half_count * half + ((place + slot) & (half_count - 1))
            source, target = ((sb0, rb0), (sb1, rb1))[a]
            return pltpu.make_async_remote_copy(
                src_ref=source.at[there],
                dst_ref=target.at[slot],
                send_sem=bs_sem.at[a, slot],
                recv_sem=br_sem.at[a, slot],
                device_id=(lat, there),
                device_id_type=MESH,
            )

        def keep_copy(a):
            source, target = ((sb0, rb0), (sb1, rb1))[a]
            return pltpu.make_async_copy(source.at[lon], target.at[0], keep_sem.at[3 + a])

        def send_bias(a, i):
            for slot in range(1, half_count) if i else range(half_count, lon_count):
                bias_copy(a, slot).start()
            if i:
                keep_copy(a).start()

        def arrived(g):
            for copy in own_copies[g] + halo_copies[g]:
                copy.wait()

        def run(*pieces):
            for piece in pieces:
                next(piece)

        p0, p1, f0, f1 = prepare(0), prepare(1), finish(0), finish(1)
        b0, b1, b2, b3 = (block(0, i, c) for i in range(2) for c in range(2))
        b4, b5, b6, b7 = (block(1, i, c) for i in range(2) for c in range(2))
        arrived(0)
        run(*[p0] * 6)
        run(b0, b1)
        arrived(1)
        run(p1, p1, b0, p1, b2, b1, p1, b3, b0, p1, b2, b1, p1)
        pack(0, 0)
        send_bias(0, 0)
        run(b4, b3, b2, b5, b4, b3)
        pack(0, 1)
        send_bias(0, 1)
        run(b6, f0, b5, b7, b4, b6, f0)
        grad_copies = send_grads(0)
        run(b5, b7, b6, b7, f1, f1)
        grad_copies += send_grads(1)
        pack(1, 0)
        pack(1, 1)
        send_bias(1, 0)
        send_bias(1, 1)

        for copy in grad_copies:
            copy.wait()
        for a in range(2):
            keep_copy(a).wait()

        for a in range(2):
            for slot in range(1, lon_count):
                bias_copy(a, slot).wait()

    return kernel


def make_final(lon_count):
    def final(rb0, rb1, gr, near, edge, out_ref, bout_ref):
        lane = iota((1, 128), 1) < 64
        out_ref[:, 3:6, 1:3] = near[:, :, 1:3]
        out_ref[:, 3:6, 0] = near[:, :, 0] + edge[...]
        back = one_hot(iota((72, 80), 0) == far_place(iota((72, 80), 1)))
        for a in range(2):
            for l in range(2):
                rows = nn(back, split(gr.at[a], l))
                out_ref[(2 * a + l + 1) % 4, 0:3] = rows.reshape(3, 3, 8, C).astype(BF)
        sum0, sum1 = rb0[0].astype(F32), rb1[0].astype(F32)
        for slot in range(1, lon_count):
            sum0 += rb0[slot].astype(F32)
            sum1 += rb1[slot].astype(F32)
        first = jnp.concatenate([sum0, pltpu.roll(sum0, 64, 1)], axis=0)
        second = jnp.concatenate([pltpu.roll(sum1, 64, 1), sum1[8:40]], axis=0)
        early = lax.axis_index("lon") < lon_count // 2
        second = jnp.concatenate(
            [jnp.where(early, second, 0.0), jnp.where(early, 0.0, second)], axis=0
        )
        both = jnp.where(lane, first, second).T
        for a in range(2):
            for h in range(HEADS):
                for q in range(9):
                    at = 64 * a + 9 * h + q
                    bout_ref[a, h, q] = both[at : at + 1]

    return final


def make_local(lat_count, lon_count):
    def local(tokens, cotangent, norm_gain, inproj_weight, outproj_weight, bias):
        any_spec = pl.BlockSpec(memory_space=pl.ANY)
        vmem = pl.BlockSpec(memory_space=pltpu.VMEM)
        dma = pltpu.SemaphoreType.DMA
        parts = pl.pallas_call(
            make_kernel(lat_count, lon_count),
            out_shape=(
                pltpu.VMEM((OWNERS, 72, 128), BF),
                pltpu.VMEM((OWNERS, 40, 128), BF),
                pltpu.VMEM((2, 3, 10, 8, 128), BF),
                pltpu.VMEM((4, 3, 3, 8, C), BF),
                pltpu.VMEM((4, 3, 8, C), BF),
            ),
            in_specs=[any_spec] * 6,
            out_specs=(any_spec,) * 5,
            scratch_shapes=[
                pltpu.VMEM((2, 4, 3, 4, 8, C), BF),
                pltpu.VMEM((2, 4, 3, 3, 8, C), BF),
                pltpu.VMEM((4, 3, 10, 8, 128), BF),
                pltpu.VMEM((4, 3, 10, 8, 128), BF),
                pltpu.VMEM((80, 72), BF),
                pltpu.VMEM((2, 3, 10, 8, 128), BF),
                pltpu.VMEM((2, 864, 144), F32),
                pltpu.VMEM((2, 144, HALF), F32),
                pltpu.VMEM((2, 72, HALF), F32),
                pltpu.VMEM((128 * HEADS, HALF), BF),
                pltpu.VMEM((72 * HEADS, HALF), BF),
                pltpu.VMEM((72, HALF), BF),
                pltpu.VMEM((C, HALF), BF),
                pltpu.VMEM((144, 176), BF),
                pltpu.VMEM((176, 144), BF),
                pltpu.VMEM((1, C), F32),
                pltpu.VMEM((C, 3 * C), BF),
                pltpu.VMEM((C, C), BF),
            ]
            + [pltpu.VMEM((C, C), BF)] * 3
            + [
                pltpu.VMEM((2 * C, C), BF),
                pltpu.VMEM((2, 2, 144, C), F32),
                pltpu.VMEM((2, 2, 144, 1), F32),
                pltpu.VMEM((2, 2, 2, C, HALF), BF),
                pltpu.VMEM((2, 2, 2, C, HALF), BF),
                pltpu.VMEM((6, 144, C), BF),
                pltpu.VMEM((6, 144, C), BF),
                pltpu.VMEM((6, C, 144), BF),
                pltpu.VMEM((2, 2, 2, 72, C), F32),
                pltpu.VMEM((2, 2, 2, 72, C), F32),
                pltpu.VMEM((2, 2, 2, 72, C), F32),
                pltpu.VMEM((4, 3, 4, 8, C), BF),
                pltpu.VMEM((OWNERS, 72, 128), BF),
                pltpu.VMEM((OWNERS, 40, 128), BF),
                dma((5,)),
                dma((2, 2, 3)),
                dma((2, 3)),
                dma((2, 3)),
                dma((2, 2)),
                dma((2, 2)),
                dma((2, OWNERS)),
                dma((2, OWNERS)),
                dma((3, 3)),
                dma((3, 3)),
                dma((5,)),
            ],
            compiler_params=pltpu.CompilerParams(collective_id=0, has_side_effects=True),
        )(
            tokens.reshape(4, 6, 3, 8, C),
            cotangent.reshape(4, 6, 3, 8, C),
            norm_gain.reshape(1, C),
            inproj_weight,
            outproj_weight,
            bias.reshape(2, 864, 144),
        )
        grad, bias_grad = pl.pallas_call(
            make_final(lon_count),
            out_shape=(
                jax.ShapeDtypeStruct((4, 6, 3, 8, C), BF),
                jax.ShapeDtypeStruct((2, HEADS, 9, 1, 144), F32),
            ),
            in_specs=[vmem] * 5,
            out_specs=(vmem, vmem),
            compiler_params=pltpu.CompilerParams(vmem_limit_bytes=8 * 1024 * 1024),
        )(*parts)
        return grad.reshape(4, 6, 24, C), bias_grad.reshape(2, 1, HEADS, 9, 144)

    return local


def solution(mesh):
    placed = (
        P(None, "lat", "lon", None),
        P(None, "lat", "lon", None),
        P(),
        P(),
        P(),
        P(None, "lat", None, None, None),
    )
    return jax.shard_map(
        make_local(mesh.shape["lat"], mesh.shape["lon"]),
        mesh=mesh,
        in_specs=placed,
        out_specs=(P(None, "lat", "lon", None), P(None, "lat", None, "lon", None)),
        check_vma=False,
    )
```

```python
import jax
import jax.numpy as jnp
from jax import lax
from jax.experimental import pallas as pl
from jax.experimental.pallas import tpu as pltpu
from jax.sharding import PartitionSpec as P

EPS = 1e-05
HEADS = 6
C = 192
LOG2E = 1.4426950408889634
LN2 = 0.6931471805599453
SCALE = 32 ** (-0.5)
BF = jnp.bfloat16
F32 = jnp.float32
OWNERS = 16
HALF = 512
GROUPS = ((1, 0, 2), (3, 2, 1), (0, 3, 1))
MESH = pl.DeviceIdType.MESH


def nn(a, b):
    return lax.dot_general(a, b, (((1,), (0,)), ((), ())), preferred_element_type=F32)


def nt(a, b):
    return lax.dot_general(a, b, (((1,), (1,)), ((), ())), preferred_element_type=F32)


def tn(a, b):
    return lax.dot_general(a, b, (((0,), (0,)), ((), ())), preferred_element_type=F32)


def iota(shape, dim):
    return lax.broadcasted_iota(jnp.int32, shape, dim)


def one_hot(cond):
    return jnp.where(cond, 1.0, 0.0).astype(BF)


def lane_head():
    return ((iota((1, HALF), 1) & 63) * 57) >> 9


def lane_query():
    lane = iota((1, HALF), 1)
    return 9 * (lane >> 6) + (lane & 63) - 9 * lane_head()


def far_place(e):
    row = (e * 57) >> 10
    d = e - 56
    edge_row = (d * 43) >> 8
    return jnp.where(
        e < 54,
        24 * row + 6 + e - 18 * row,
        jnp.where((d >= 0) & (d < 18), 24 * edge_row + d - 6 * edge_row, -1),
    )


def join(one, two):
    tail = jnp.concatenate([one[:, 128:192], two[:, 128:192]], axis=1)
    return [v.astype(BF).reshape(10, 8, 128) for v in (one[:, 0:128], two[:, 0:128], tail)]


def split(ref, which):
    return jnp.concatenate(
        [ref[which].reshape(80, 128), ref[2].reshape(80, 128)[:, 64 * which : 64 * which + 64]], axis=1
    )


def make_kernel(lat_count, lon_count):
    def kernel(
        tok, cot, gain_hbm, win_hbm, wout_hbm, bias_ref, rb0, rb1, gr, near, edge,
        x, far, fs, fr, ps, gs, bias_v, bt0, bt1, perm, permb, choose, mask, pcs, pct,
        gain_ref, win_ref, wout_ref, wq, wk, wv, wqkt,
        standard, inverse, qbd, ubd, keys, vals, keyt, gq, gk, gv, ext, sb0, sb1,
        in_sem, own_sem, hs_sem, hr_sem, fs_sem, fr_sem, bs_sem, br_sem, gs_sem, gr_sem, keep_sem,
    ):
        lat = lax.axis_index("lat")
        lon = lax.axis_index("lon")
        half_count = lon_count // 2
        own_half = lon // half_count
        place = lax.rem(lon, half_count)
        other_half = 1 - own_half
        lat_next = lax.rem(lat + 1, lat_count)
        lat_prev = lax.rem(lat + lat_count - 1, lat_count)
        lon_next = lax.rem(lon + 1, lon_count)
        lon_prev = lax.rem(lon + lon_count - 1, lon_count)

        barrier = pltpu.get_barrier_semaphore()

        def greet(r, carry):
            pl.semaphore_signal(
                barrier, inc=1, device_id=(lat, lax.rem(lon + r, lon_count)), device_id_type=MESH
            )
            return carry

        for there in ((lat_prev, lon), (lat_next, lon), (lat_prev, lon_prev), (lat_next, lon_next)):
            pl.semaphore_signal(barrier, inc=1, device_id=there, device_id_type=MESH)
        lax.fori_loop(1, lon_count, greet, 0)

        own_copies, far_copies = [[], []], []
        for g, (src, z, count) in enumerate(GROUPS):
            for which, ref in enumerate((tok, cot)):
                copy = pltpu.make_async_copy(
                    ref.at[src : src + count, 0:3], far.at[which, z : z + count], own_sem.at[1, which, g]
                )
                copy.start()
                far_copies.append(copy)
        for g, (src, z, count) in enumerate(GROUPS):
            for which, ref in enumerate((tok, cot)):
                copy = pltpu.make_async_copy(
                    ref.at[src : src + count, 3:6],
                    x.at[which, z : z + count, :, 0:3],
                    own_sem.at[0, which, g],
                )
                copy.start()
                own_copies[min(g, 1)].append(copy)
        in_copies = [
            pltpu.make_async_copy(source, target, in_sem.at[i])
            for i, (source, target) in enumerate(
                (
                    (bias_ref.at[0], bias_v.at[0]),
                    (bias_ref.at[1], bias_v.at[1]),
                    (win_hbm, win_ref),
                    (wout_hbm, wout_ref),
                    (gain_hbm, gain_ref),
                )
            )
        ]
        for copy in in_copies:
            copy.start()

        ps[...] = one_hot(iota((80, 72), 1) == far_place(iota((80, 72), 0)))
        for copy in far_copies:
            copy.wait()
        for z in range(4):
            one, two = (nn(ps[...], far[which, z].reshape(72, C)) for which in range(2))
            for i, v in enumerate(join(one, two)):
                fs[z, i] = v

        pl.semaphore_wait(barrier, lon_count - 1 + 4)

        halo_copies = [[], []]
        for a in range(2):
            span = pl.ds(2 * a, 2)
            pieces = [
                (fs.at[span, :, 7:10], fr.at[span, :, 7:10], (lat_prev, lon_prev), fs_sem.at[a, 0], fr_sem.at[a, 0]),
                (fs.at[span, :, 0:7], fr.at[span, :, 0:7], (lat_prev, lon), fs_sem.at[a, 1], fr_sem.at[a, 1]),
            ]
            for g in ((1, 2) if a else (0,)):
                src, z, count = GROUPS[g]
                for which, ref in enumerate((tok, cot)):
                    pieces.append(
                        (
                            ref.at[src : src + count, 3:6, 0],
                            x.at[which, z : z + count, :, 3],
                            (lat, lon_prev),
                            hs_sem.at[which, g],
                            hr_sem.at[which, g],
                        )
                    )
            for source, target, there, send_sem, recv_sem in pieces:
                copy = pltpu.make_async_remote_copy(
                    src_ref=source,
                    dst_ref=target,
                    send_sem=send_sem,
                    recv_sem=recv_sem,
                    device_id=there,
                    device_id_type=MESH,
                )
                copy.start()
                halo_copies[a].append(copy)

        heads, queries = lane_head(), lane_query()
        perm[...] = one_hot(iota((128 * HEADS, HALF), 0) == 128 * heads + queries)
        permb[...] = one_hot(iota((72 * HEADS, HALF), 0) == 72 * heads + queries)
        choose[...] = one_hot((iota((72, HALF), 0) == queries) & (heads < HEADS))
        mask[...] = one_hot((iota((C, HALF), 0) >> 5) == heads)
        def grid_place(token):
            c = (token >= 72).astype(jnp.int32)
            inside = token - 72 * c
            row = (inside * 43) >> 9
            col = inside - 12 * row + 6 + 12 * c
            return jnp.where(
                row < 3,
                32 * row + col,
                96 + jnp.where(col < 24, 18 * row + col - 60, 6 * row + col + 14),
            )

        pcs[...] = one_hot(iota((144, 176), 1) == grid_place(iota((144, 176), 0)))
        pct[...] = one_hot(iota((176, 144), 0) == grid_place(iota((176, 144), 1)))
        for copy in in_copies:
            copy.wait()
        wq[...] = win_ref[:, 0:192]
        wk[...] = win_ref[:, 192:384]
        wv[...] = win_ref[:, 384:576]
        wqkt[0:192] = wq[...].astype(F32).T.astype(BF)
        wqkt[192:384] = wk[...].astype(F32).T.astype(BF)

        is_last = jnp.where(lat == lat_count - 1, -1e30, 0.0).astype(F32)
        query_late = queries >= 36

        def penalty(rows):
            return jnp.where((lax.rem(iota((rows, 1), 0), 72) >= 36) != query_late, is_last, 0.0)

        for a in range(2):
            for s in range(2):
                b = LOG2E * jnp.concatenate(
                    [bias_v[a, 144 * h + 72 * s : 144 * h + 72 * s + 72, :] for h in range(HEADS)], axis=0
                )
                high = b.astype(BF)
                low = (b - high.astype(F32)).astype(BF)
                moved = tn(high, permb[...]) + tn(low, permb[...])
                if a == 0:
                    bt0[s] = moved + penalty(144)
                else:
                    bt1[s] = moved[72 * s : 72 * s + 72] + penalty(72)

        gain = gain_ref[...]
        lane = iota((1, 128), 1) < 64
        blank = jnp.zeros((56, C), F32)

        def pad_pair(v):
            return jnp.concatenate([v[0:72], blank, v[72:144], blank], axis=0).astype(BF)

        def compact(sides):
            return jnp.concatenate(
                [
                    jnp.concatenate(
                        [side[32 * h : 32 * h + 32, 128 * c : 128 * c + 128] for h in range(HEADS)], axis=1
                    )
                    for side in sides
                    for c in range(2)
                ],
                axis=0,
            )

        def expand(target, wide):
            for l in range(2):
                for c in range(2):
                    at = 32 * (2 * l + c)
                    target[l, c] = jnp.concatenate([wide[at : at + 32]] * HEADS, axis=0) * mask[...]

        def prepare(a):
            ts, cts = (
                [
                    nn(
                        pcs[...],
                        jnp.concatenate(
                            [x[which, 2 * a + l].reshape(96, C), split(fr.at[2 * a + l], which)], axis=0
                        ),
                    )
                    for l in range(2)
                ]
                for which in range(2)
            )
            yield
            uts = [nt(wout_ref[...], pad_pair(cts[l])).astype(BF) for l in range(2)]
            plain = []
            for l in range(2):
                centred = ts[l] - jnp.sum(ts[l], axis=-1, keepdims=True) * (1.0 / C)
                inv = lax.rsqrt(jnp.sum(centred * centred, axis=-1, keepdims=True) * (1.0 / C) + EPS)
                unit = centred * inv
                inverse[a, l] = inv
                standard[a, l] = unit
                plain.append(unit * gain)
            yield
            expand(ubd.at[a], nn(compact(uts), perm[...]).astype(BF))
            yield
            qts = []
            for l in range(2):
                projected = nt(wqkt[...] if a else wqkt[0:192], pad_pair(plain[l]))
                qts.append((projected[0:192] * (SCALE * LOG2E)).astype(BF))
                if a:
                    for c in range(2):
                        keyt[2 + 2 * l + c, :, 0:72] = (
                            projected[192:384, 128 * c : 128 * c + 72] * SCALE
                        ).astype(BF)
            yield
            together = jnp.concatenate(plain, axis=0).astype(BF)
            for target, weight in ((keys, wk), (vals, wv)):
                rows = nn(together, weight[...])
                for c in range(2):
                    if a:
                        for l in range(2):
                            at = 144 * l + 72 * c
                            target[2 + 2 * l + c, 0:72] = rows[at : at + 72].astype(BF)
                    else:
                        target[c] = jnp.concatenate(
                            [rows[72 * c : 72 * c + 72], rows[144 + 72 * c : 216 + 72 * c]], axis=0
                        ).astype(BF)
            if not a:
                for c in range(2):
                    whole = jnp.concatenate([v[72 * c : 72 * c + 72] for v in plain], axis=0).astype(BF)
                    keyt[c] = (nt(wqkt[192:384], whole) * SCALE).astype(BF)
            yield
            expand(qbd.at[a], nn(compact(qts), perm[...]).astype(BF))
            yield

        sums = {}
        parts = {}

        halves = (other_half, own_half)

        def block(a, i, c):
            s = halves[i]
            if a:
                at = 2 + 2 * s + c
                k, v, kt, biast = keys[at, 0:72], vals[at, 0:72], keyt[at, :, 0:72], bt1[s]
            else:
                k, v, kt, biast = keys[c], vals[c], keyt[c], bt0[s]
            scores = nn(k, qbd[a, s, c])
            dprobs = nn(v, ubd[a, s, c])
            yield
            e = jnp.exp2(scores + biast)
            probs = e * (1.0 / jnp.sum(e, axis=0, keepdims=True))
            weighted = probs * dprobs
            dscores = weighted - probs * jnp.sum(weighted, axis=0, keepdims=True)
            sums[a, i] = dscores if c == 0 else sums[a, i] + dscores
            low = dscores.astype(BF)
            dv = nt(probs.astype(BF), ubd[a, s, c])
            wide = nn(kt, low)
            dk = nt(low, qbd[a, s, c]) * LN2
            if a:
                gk[a, s, c] = dk
                gv[a, s, c] = dv
            elif i == 0:
                parts[c] = (dk, dv)
            else:
                for target, total in ((gk, parts[c][0] + dk), (gv, parts[c][1] + dv)):
                    for l in range(2):
                        target[a, l, c] = total[72 * l : 72 * l + 72]
            yield
            gq[a, s, c] = nt(choose[...], wide.astype(BF) * mask[...])
            yield

        def pack(a, i):
            for tile in range(4):
                part = sums[a, i][:, 128 * tile : 128 * tile + 128]
                target, top, bottom = (sb1, part[0:40], part[32:72]) if a else (sb0, part[0:72], part[72:144])
                owner = 8 * halves[i] + 2 * tile
                target[owner] = jnp.where(lane, top, pltpu.roll(bottom, 64, 1)).astype(BF)
                target[owner + 1] = jnp.where(lane, pltpu.roll(top, 64, 1), bottom).astype(BF)

        def finish(a):
            dq, dk, dv = (ref[a].reshape(288, C).astype(BF) for ref in (gq, gk, gv))
            scaled = (nt(dq, wq[...]) + nt(dk, wk[...]) + nt(dv, wv[...])) * gain
            yield
            away = []
            for l in range(2):
                part = scaled[144 * l : 144 * l + 144]
                unit = standard[a, l]
                grad = inverse[a, l] * (
                    part
                    - jnp.sum(part, axis=-1, keepdims=True) * (1.0 / C)
                    - unit * (jnp.sum(part * unit, axis=-1, keepdims=True) * (1.0 / C))
                )
                full = nn(pct[...], grad.astype(BF))
                ext[(2 * a + l + 1) % 4] = full[0:96].reshape(3, 4, 8, C).astype(BF)
                away.append(full[96:176])
            for i, v in enumerate(join(*away)):
                gs[a, i] = v
            yield

        def send_grads(a):
            pieces = [
                (gs.at[a, :, 0:7], gr.at[a, :, 0:7], (lat_next, lon), gs_sem.at[a, 0], gr_sem.at[a, 0]),
                (gs.at[a, :, 7:10], gr.at[a, :, 7:10], (lat_next, lon_next), gs_sem.at[a, 1], gr_sem.at[a, 1]),
            ]
            copies = []
            for g in ((1, 2) if a else (0,)):
                level, _, count = GROUPS[g]
                span = pl.ds(level, count)
                pieces.append(
                    (ext.at[span, :, 3], edge.at[span], (lat, lon_next), gs_sem.at[2, g], gr_sem.at[2, g])
                )
                copies.append(pltpu.make_async_copy(ext.at[span, :, 0:3], near.at[span], keep_sem.at[g]))
            copies = [
                pltpu.make_async_remote_copy(
                    src_ref=source,
                    dst_ref=target,
                    send_sem=send_sem,
                    recv_sem=recv_sem,
                    device_id=there,
                    device_id_type=MESH,
                )
                for source, target, there, send_sem, recv_sem in pieces
            ] + copies
            for copy in copies:
                copy.start()
            return copies

        def bias_copy(a, slot):
            half = other_half if slot >= half_count else own_half
            there = half_count * half + ((place + slot) & (half_count - 1))
            source, target = ((sb0, rb0), (sb1, rb1))[a]
            return pltpu.make_async_remote_copy(
                src_ref=source.at[there],
                dst_ref=target.at[slot],
                send_sem=bs_sem.at[a, slot],
                recv_sem=br_sem.at[a, slot],
                device_id=(lat, there),
                device_id_type=MESH,
            )

        def keep_copy(a):
            source, target = ((sb0, rb0), (sb1, rb1))[a]
            return pltpu.make_async_copy(source.at[lon], target.at[0], keep_sem.at[3 + a])

        def send_bias(a, i):
            for slot in range(1, half_count) if i else range(half_count, lon_count):
                bias_copy(a, slot).start()
            if i:
                keep_copy(a).start()

        def arrived(g):
            for copy in own_copies[g] + halo_copies[g]:
                copy.wait()

        def run(*pieces):
            for piece in pieces:
                next(piece)

        p0, p1, f0, f1 = prepare(0), prepare(1), finish(0), finish(1)
        b0, b1, b2, b3 = (block(0, i, c) for i in range(2) for c in range(2))
        b4, b5, b6, b7 = (block(1, i, c) for i in range(2) for c in range(2))
        arrived(0)
        run(*[p0] * 6)
        run(b0, b1, b0, b2, b1, b3)
        pack(0, 0)
        send_bias(0, 0)
        arrived(1)
        run(b2, p1, b3, p1)
        pack(0, 1)
        send_bias(0, 1)
        run(b0, p1, b1, p1, b2, p1, b3, p1)
        run(b4, b6, f0, b5, b4, b6, b7, b5, f0)
        grad_copies = send_grads(0)
        run(b4, b7, b5, b6, b7, f1, f1)
        grad_copies += send_grads(1)
        pack(1, 0)
        pack(1, 1)
        send_bias(1, 0)
        send_bias(1, 1)

        for copy in grad_copies:
            copy.wait()
        for a in range(2):
            keep_copy(a).wait()

        for a in range(2):
            for slot in range(1, lon_count):
                bias_copy(a, slot).wait()

    return kernel


def make_final(lon_count):
    def final(rb0, rb1, gr, near, edge, out_ref, bout_ref):
        lane = iota((1, 128), 1) < 64
        out_ref[:, 3:6, 1:3] = near[:, :, 1:3]
        out_ref[:, 3:6, 0] = near[:, :, 0] + edge[...]
        back = one_hot(iota((72, 80), 0) == far_place(iota((72, 80), 1)))
        for a in range(2):
            for l in range(2):
                rows = nn(back, split(gr.at[a], l))
                out_ref[(2 * a + l + 1) % 4, 0:3] = rows.reshape(3, 3, 8, C).astype(BF)
        sum0, sum1 = rb0[0].astype(F32), rb1[0].astype(F32)
        for slot in range(1, lon_count):
            sum0 += rb0[slot].astype(F32)
            sum1 += rb1[slot].astype(F32)
        first = jnp.concatenate([sum0, pltpu.roll(sum0, 64, 1)], axis=0)
        second = jnp.concatenate([pltpu.roll(sum1, 64, 1), sum1[8:40]], axis=0)
        early = lax.axis_index("lon") < lon_count // 2
        second = jnp.concatenate(
            [jnp.where(early, second, 0.0), jnp.where(early, 0.0, second)], axis=0
        )
        both = jnp.where(lane, first, second).T
        for a in range(2):
            for h in range(HEADS):
                for q in range(9):
                    at = 64 * a + 9 * h + q
                    bout_ref[a, h, q] = both[at : at + 1]

    return final


def make_local(lat_count, lon_count):
    def local(tokens, cotangent, norm_gain, inproj_weight, outproj_weight, bias):
        any_spec = pl.BlockSpec(memory_space=pl.ANY)
        vmem = pl.BlockSpec(memory_space=pltpu.VMEM)
        dma = pltpu.SemaphoreType.DMA
        parts = pl.pallas_call(
            make_kernel(lat_count, lon_count),
            out_shape=(
                pltpu.VMEM((OWNERS, 72, 128), BF),
                pltpu.VMEM((OWNERS, 40, 128), BF),
                pltpu.VMEM((2, 3, 10, 8, 128), BF),
                pltpu.VMEM((4, 3, 3, 8, C), BF),
                pltpu.VMEM((4, 3, 8, C), BF),
            ),
            in_specs=[any_spec] * 6,
            out_specs=(any_spec,) * 5,
            scratch_shapes=[
                pltpu.VMEM((2, 4, 3, 4, 8, C), BF),
                pltpu.VMEM((2, 4, 3, 3, 8, C), BF),
                pltpu.VMEM((4, 3, 10, 8, 128), BF),
                pltpu.VMEM((4, 3, 10, 8, 128), BF),
                pltpu.VMEM((80, 72), BF),
                pltpu.VMEM((2, 3, 10, 8, 128), BF),
                pltpu.VMEM((2, 864, 144), F32),
                pltpu.VMEM((2, 144, HALF), F32),
                pltpu.VMEM((2, 72, HALF), F32),
                pltpu.VMEM((128 * HEADS, HALF), BF),
                pltpu.VMEM((72 * HEADS, HALF), BF),
                pltpu.VMEM((72, HALF), BF),
                pltpu.VMEM((C, HALF), BF),
                pltpu.VMEM((144, 176), BF),
                pltpu.VMEM((176, 144), BF),
                pltpu.VMEM((1, C), F32),
                pltpu.VMEM((C, 3 * C), BF),
                pltpu.VMEM((C, C), BF),
            ]
            + [pltpu.VMEM((C, C), BF)] * 3
            + [
                pltpu.VMEM((2 * C, C), BF),
                pltpu.VMEM((2, 2, 144, C), F32),
                pltpu.VMEM((2, 2, 144, 1), F32),
                pltpu.VMEM((2, 2, 2, C, HALF), BF),
                pltpu.VMEM((2, 2, 2, C, HALF), BF),
                pltpu.VMEM((6, 144, C), BF),
                pltpu.VMEM((6, 144, C), BF),
                pltpu.VMEM((6, C, 144), BF),
                pltpu.VMEM((2, 2, 2, 72, C), F32),
                pltpu.VMEM((2, 2, 2, 72, C), F32),
                pltpu.VMEM((2, 2, 2, 72, C), F32),
                pltpu.VMEM((4, 3, 4, 8, C), BF),
                pltpu.VMEM((OWNERS, 72, 128), BF),
                pltpu.VMEM((OWNERS, 40, 128), BF),
                dma((5,)),
                dma((2, 2, 3)),
                dma((2, 3)),
                dma((2, 3)),
                dma((2, 2)),
                dma((2, 2)),
                dma((2, OWNERS)),
                dma((2, OWNERS)),
                dma((3, 3)),
                dma((3, 3)),
                dma((5,)),
            ],
            compiler_params=pltpu.CompilerParams(collective_id=0, has_side_effects=True),
        )(
            tokens.reshape(4, 6, 3, 8, C),
            cotangent.reshape(4, 6, 3, 8, C),
            norm_gain.reshape(1, C),
            inproj_weight,
            outproj_weight,
            bias.reshape(2, 864, 144),
        )
        grad, bias_grad = pl.pallas_call(
            make_final(lon_count),
            out_shape=(
                jax.ShapeDtypeStruct((4, 6, 3, 8, C), BF),
                jax.ShapeDtypeStruct((2, HEADS, 9, 1, 144), F32),
            ),
            in_specs=[vmem] * 5,
            out_specs=(vmem, vmem),
            compiler_params=pltpu.CompilerParams(vmem_limit_bytes=8 * 1024 * 1024),
        )(*parts)
        return grad.reshape(4, 6, 24, C), bias_grad.reshape(2, 1, HEADS, 9, 144)

    return local


def solution(mesh):
    placed = (
        P(None, "lat", "lon", None),
        P(None, "lat", "lon", None),
        P(),
        P(),
        P(),
        P(None, "lat", None, None, None),
    )
    return jax.shard_map(
        make_local(mesh.shape["lat"], mesh.shape["lon"]),
        mesh=mesh,
        in_specs=placed,
        out_specs=(P(None, "lat", "lon", None), P(None, "lat", None, "lon", None)),
        check_vma=False,
    )
```
